32 devices in a mesh: lat: 4 (over y, x), lon: 8 (over z, core).
Axes of the slice: x: 2, y: 2, z: 4, core: 2. Of those that a mesh axis runs over, the one named last changes fastest.
Arguments:
- fine_field: bfloat16 [4, 48, 96, 512], P(None, 'lat', 'lon'), may hold values from -6 to 6
- offsets: int32 [4], replicated, may hold values from 1 to 11, as said below
- fine_prenorm: float32 [512], replicated, may hold values from 0.25 to 1.75
- fine_triple: bfloat16 [512, 1536], replicated, may hold values from -0.25 to 0.25
- fine_bias: float32 [16, 144, 144], replicated, may hold values from -160 to 160
- fine_output: bfloat16 [512, 512], replicated, may hold values from -0.25 to 0.25
- fine_midnorm: float32 [512], replicated, may hold values from 0.25 to 1.75
- fine_expand: bfloat16 [512, 2048], replicated, may hold values from -0.25 to 0.25
- fine_reduce: bfloat16 [2048, 512], replicated, may hold values from -0.125 to 0.125
- merge_gain: float32 [2048], replicated, may hold values from 0.25 to 1.75
- merge_weight: bfloat16 [2048, 1024], replicated, may hold values from -0.125 to 0.125
- coarse_prenorm: float32 [1024], replicated, may hold values from 0.25 to 1.75
- coarse_triple: bfloat16 [1024, 3072], P(None, 'lon'), may hold values from -0.1875 to 0.1875
- coarse_bias: float32 [32, 144, 144], P('lon'), may hold values from -160 to 160
- coarse_output: bfloat16 [1024, 1024], P('lon'), may hold values from -0.1875 to 0.1875
- coarse_midnorm: float32 [1024], replicated, may hold values from 0.25 to 1.75
- coarse_expand: bfloat16 [1024, 4096], P(None, 'lon'), may hold values from -0.1875 to 0.1875
- coarse_reduce: bfloat16 [4096, 1024], P('lon'), may hold values from -0.09375 to 0.09375
- upsample_weight: bfloat16 [1024, 2048], replicated, may hold values from -0.1875 to 0.1875
Outputs:
- blended: bfloat16 [4, 48, 96, 512], P(None, 'lat', 'lon')
- coarse_state: bfloat16 [4, 24, 48, 1024], P(None, 'lat', 'lon')
The draws below stay inside these ranges and needn't reach their ends.
Inputs may be any that keep to these rules, and one draw needn't show every extreme that they name: `offsets`: entries 0 and 2 lie in 1 to 5, entries 1 and 3 in 1 to 11; in every draw entry 0 or entry 2 equals 5, and entry 1 or entry 3 equals 11.
All inputs are finite; a program needn't handle non-finite values.
Results may differ from the reference program's by a relative error of at most 0.024.
Values may be sent and summed in bfloat16 or wider, within the bound.
A program may use at most 128 MiB of HBM per device.

```python
import jax
import jax.numpy as jnp
from jax import lax

C1 = 512
H1 = 16
C2 = 1024
H2 = 32
DEP = 4
WD = 2
WL = 6
WW = 12
WT = 144
FF1 = 2048
FF2 = 4096
HF = 48
WG = 96
WC = 48
N_LON = 8


def pair_score_table(key, head_count):
    base_vals = jnp.clip(jax.random.normal(key, (head_count, WT, WT), jnp.float32), -4.0, 4.0)
    return base_vals


def draw_fine_bias(key, part):
    return pair_score_table(jax.random.fold_in(key, 11), H1)


def draw_coarse_bias(key, part):
    return pair_score_table(jax.random.fold_in(key, 13), H2)


def draw_offsets(key, part):
    key_list = jax.random.split(jax.random.fold_in(key, 3), 4)
    lat_other = jax.random.randint(key_list[0], (), 1, WL)
    lon_other = jax.random.randint(key_list[1], (), 1, WW)
    lat_side = jax.random.randint(key_list[2], (), 0, 2)
    lon_side = jax.random.randint(key_list[3], (), 0, 2)
    lat_most = jnp.full((), WL - 1, jnp.int32)
    lon_most = jnp.full((), WW - 1, jnp.int32)
    fine_lat = jnp.where(lat_side == 0, lat_most, lat_other)
    coarse_lat = jnp.where(lat_side == 0, lat_other, lat_most)
    fine_lon = jnp.where(lon_side == 0, lon_most, lon_other)
    coarse_lon = jnp.where(lon_side == 0, lon_other, lon_most)
    return jnp.stack([fine_lat, fine_lon, coarse_lat, coarse_lon]).astype(jnp.int32)


def shard_levels(rng, extent, shards, low, high):
    factor_of = 1.0
    for position, shards_of in shards:
        heights = jax.random.uniform(jax.random.fold_in(jax.random.fold_in(rng, 6), position), (shards_of,), jnp.float32, low / len(shards), high / len(shards))
        factor_of = factor_of * jnp.repeat(jnp.exp(heights), extent[position] // shards_of).reshape((-1,) + (1,) * (len(extent) - 1 - position))
    return factor_of


def gaussian(rng, shape, scale, limit, cuts=(), kind=jnp.bfloat16):
    level = shard_levels(rng, shape, cuts, -0.22, 0.18) if cuts else 1.0
    drawn = jax.random.normal(rng, shape, jnp.float32) * scale * level
    return jnp.minimum(jnp.maximum(drawn, -limit), limit).astype(kind)


def setup_inputs(seed: int = 0) -> dict:
    arg_keys = jax.random.split(jax.random.key(seed), 20)
    fine_field = gaussian(arg_keys[0], (DEP, HF, WG, C1), 1.0, 6.0, ((1, 4), (2, 8)))
    offsets = draw_offsets(jax.random.fold_in(arg_keys[19], 71), 0)
    fine_prenorm = jnp.clip(1.0 + 0.15 * jax.random.normal(arg_keys[2], (C1,), jnp.float32), 0.25, 1.75)
    fine_triple = gaussian(arg_keys[3], (C1, 3 * C1), C1 ** -0.5, 0.25)
    fine_bias = draw_fine_bias(jax.random.fold_in(arg_keys[19], 71), 0)
    fine_output = gaussian(arg_keys[5], (C1, C1), C1 ** -0.5, 0.25)
    fine_midnorm = jnp.clip(1.0 + 0.15 * jax.random.normal(arg_keys[6], (C1,), jnp.float32), 0.25, 1.75)
    fine_expand = gaussian(arg_keys[7], (C1, FF1), C1 ** -0.5, 0.25)
    fine_reduce = gaussian(arg_keys[8], (FF1, C1), FF1 ** -0.5, 0.125)
    merge_gain = jnp.clip(1.0 + 0.15 * jax.random.normal(arg_keys[9], (4 * C1,), jnp.float32), 0.25, 1.75)
    merge_weight = gaussian(arg_keys[10], (4 * C1, C2), (4 * C1) ** -0.5, 0.125)
    coarse_prenorm = jnp.clip(1.0 + 0.15 * jax.random.normal(arg_keys[11], (C2,), jnp.float32), 0.25, 1.75)
    coarse_triple = gaussian(arg_keys[12], (C2, 3 * C2), C2 ** -0.5, 0.1875, ((1, 8),))
    coarse_bias = draw_coarse_bias(jax.random.fold_in(arg_keys[19], 71), 0)
    coarse_output = gaussian(arg_keys[14], (C2, C2), C2 ** -0.5, 0.1875, ((0, 8),))
    coarse_midnorm = jnp.clip(1.0 + 0.15 * jax.random.normal(arg_keys[15], (C2,), jnp.float32), 0.25, 1.75)
    coarse_expand = gaussian(arg_keys[16], (C2, FF2), C2 ** -0.5, 0.1875, ((1, 8),))
    coarse_reduce = gaussian(arg_keys[17], (FF2, C2), FF2 ** -0.5, 0.09375, ((0, 8),))
    upsample_weight = gaussian(arg_keys[18], (C2, 4 * C1), C2 ** -0.5, 0.1875)
    return dict(fine_field=fine_field, offsets=offsets, fine_prenorm=fine_prenorm, fine_triple=fine_triple, fine_bias=fine_bias, fine_output=fine_output, fine_midnorm=fine_midnorm, fine_expand=fine_expand, fine_reduce=fine_reduce, merge_gain=merge_gain, merge_weight=merge_weight, coarse_prenorm=coarse_prenorm, coarse_triple=coarse_triple, coarse_bias=coarse_bias, coarse_output=coarse_output, coarse_midnorm=coarse_midnorm, coarse_expand=coarse_expand, coarse_reduce=coarse_reduce, upsample_weight=upsample_weight)


epsilon = 1e-05
masked_score = -1e+30

def layer_norm(values, gain_vec):
    values = values.astype(jnp.float32)
    center = lax.optimization_barrier(jnp.mean(values, axis=-1, keepdims=True))
    offset_vals = values - center
    spread = lax.optimization_barrier(jnp.mean(offset_vals * offset_vals, axis=-1, keepdims=True))
    return offset_vals * lax.rsqrt(spread + epsilon) * gain_vec

def to_windows(cells_grid):
    levels, lat_rows, lon_cols, channels = cells_grid.shape
    shaped = cells_grid.reshape(levels // WD, WD, lat_rows // WL, WL, lon_cols // WW, WW, channels)
    shaped = shaped.transpose(0, 2, 4, 1, 3, 5, 6)
    return shaped.reshape(-1, WT, channels)

def from_windows(windows, levels, lat_rows, lon_cols):
    channels = windows.shape[-1]
    shaped = windows.reshape(levels // WD, lat_rows // WL, lon_cols // WW, WD, WL, WW, channels)
    return shaped.transpose(0, 3, 1, 4, 2, 5, 6).reshape(levels, lat_rows, lon_cols, channels)

def window_mix(triples, regions, bias_table):
    count_win = triples.shape[0]
    heads_all = bias_table.shape[0]
    head_dim = triples.shape[-1] // (3 * heads_all)
    parts_all = triples.astype(jnp.float32).reshape(count_win, WT, heads_all, 3, head_dim)
    queries = parts_all[:, :, :, 0]
    keys_all = parts_all[:, :, :, 1]
    values = parts_all[:, :, :, 2]
    scores = jnp.einsum('nihd,njhd->nhij', queries, keys_all) * head_dim ** (-0.5) + bias_table[None]
    allowed = regions[:, :, None] == regions[:, None, :]
    scores = jnp.where(allowed[:, None], scores, masked_score)
    row_top = lax.optimization_barrier(jnp.max(scores, axis=-1, keepdims=True))
    lifted = jnp.exp(scores - row_top)
    weights = (lifted / lax.optimization_barrier(jnp.sum(lifted, axis=-1, keepdims=True))).astype(jnp.bfloat16)
    mixed_out = jnp.einsum('nhij,njhd->nihd', weights.astype(jnp.float32), values)
    return mixed_out.astype(jnp.bfloat16).reshape(count_win, WT, heads_all * head_dim)

def shifted_attention(normed, shift_lat, shift_lon, triple_weight, bias_table):
    levels, lat_rows, lon_cols, channels = normed.shape
    rolled = jnp.roll(normed, (-shift_lat, -shift_lon), axis=(1, 2))
    triples = jnp.dot(rolled.reshape(-1, channels), triple_weight, preferred_element_type=jnp.float32).astype(jnp.bfloat16)
    triples = to_windows(triples.reshape(levels, lat_rows, lon_cols, -1))
    anchor = (jnp.arange(lat_rows, dtype=jnp.int32) + shift_lat) % lat_rows
    regions = jnp.broadcast_to((anchor < shift_lat).astype(jnp.int32)[None, :, None, None], (levels, lat_rows, lon_cols, 1))
    regions = to_windows(regions)[:, :, 0]
    item_count = levels // WD * (lat_rows // WL)
    mixed_out = lax.map(lambda operands: window_mix(operands[0], operands[1], bias_table), (triples.reshape(item_count, -1, WT, triples.shape[-1]), regions.reshape(item_count, -1, WT)))
    mixed_out = from_windows(mixed_out.reshape(-1, WT, mixed_out.shape[-1]), levels, lat_rows, lon_cols)
    return jnp.roll(mixed_out, (shift_lat, shift_lon), axis=(1, 2))

def grouped_sum(operand, weight, groups):
    inner_dim = operand.shape[-1]
    outer_dim = weight.shape[-1]
    split_weight = weight.astype(jnp.float32).reshape(groups, inner_dim // groups, outer_dim)

    def one_block(token_block):
        shaped = token_block.astype(jnp.float32).reshape(token_block.shape[0], groups, inner_dim // groups)
        partials = jnp.einsum('tgk,gkn->tgn', shaped, split_weight).astype(jnp.bfloat16)
        return lax.optimization_barrier(jnp.sum(partials.astype(jnp.float32), axis=1))
    blocks = operand.reshape(-1, WC, inner_dim)
    return lax.map(one_block, blocks).reshape(-1, outer_dim)

def reference(fine_field, offsets, fine_prenorm, fine_triple, fine_bias, fine_output, fine_midnorm, fine_expand, fine_reduce, merge_gain, merge_weight, coarse_prenorm, coarse_triple, coarse_bias, coarse_output, coarse_midnorm, coarse_expand, coarse_reduce, upsample_weight):
    levels, lat_rows, lon_cols, channels = fine_field.shape
    normed = layer_norm(fine_field, fine_prenorm).astype(jnp.bfloat16)
    mixed_out = shifted_attention(normed, offsets[0], offsets[1], fine_triple, fine_bias)
    attended = (fine_field.astype(jnp.float32).reshape(-1, channels) + jnp.dot(mixed_out.reshape(-1, channels), fine_output, preferred_element_type=jnp.float32)).astype(jnp.bfloat16)
    hidden = jax.nn.gelu(jnp.dot(layer_norm(attended, fine_midnorm).astype(jnp.bfloat16), fine_expand, preferred_element_type=jnp.float32)).astype(jnp.bfloat16)
    fine_state = (attended.astype(jnp.float32) + jnp.dot(hidden, fine_reduce, preferred_element_type=jnp.float32)).astype(jnp.bfloat16)
    fine_state = fine_state.reshape(levels, lat_rows, lon_cols, channels)
    half_rows = lat_rows // 2
    half_cols = lon_cols // 2
    merged = fine_state.reshape(levels, half_rows, 2, half_cols, 2, channels).transpose(0, 1, 3, 4, 2, 5)
    merged = merged.reshape(-1, 4 * channels)
    coarse_in = jnp.dot(layer_norm(merged, merge_gain).astype(jnp.bfloat16), merge_weight, preferred_element_type=jnp.float32).astype(jnp.bfloat16)
    wide_channels = coarse_in.shape[-1]
    normed2 = layer_norm(coarse_in, coarse_prenorm).astype(jnp.bfloat16).reshape(levels, half_rows, half_cols, wide_channels)
    mixed2 = shifted_attention(normed2, offsets[2], offsets[3], coarse_triple, coarse_bias)
    coarse_mid = (coarse_in.astype(jnp.float32) + grouped_sum(mixed2.reshape(-1, wide_channels), coarse_output, N_LON)).astype(jnp.bfloat16)
    hidden2 = jax.nn.gelu(jnp.dot(layer_norm(coarse_mid, coarse_midnorm).astype(jnp.bfloat16), coarse_expand, preferred_element_type=jnp.float32)).astype(jnp.bfloat16)
    coarse_state = (coarse_mid.astype(jnp.float32) + grouped_sum(hidden2, coarse_reduce, N_LON)).astype(jnp.bfloat16)
    expanded = jnp.dot(coarse_state, upsample_weight, preferred_element_type=jnp.float32).reshape(levels, half_rows, half_cols, 2, 2, channels)
    expanded = expanded.transpose(0, 1, 4, 2, 3, 5).reshape(levels, lat_rows, lon_cols, channels)
    blended = (fine_state.astype(jnp.float32) + expanded).astype(jnp.bfloat16)
    return (blended, coarse_state.reshape(levels, half_rows, half_cols, wide_channels))
```

```python
import functools

import jax
import jax.numpy as jnp
from jax import lax
from jax.experimental import pallas as pl
from jax.experimental.pallas import tpu as pltpu
from jax.sharding import PartitionSpec as P

WD = 2
WL = 6
WW = 12
WT = 144
HALO = WL - 1

epsilon = 1e-05
masked_score = -1e30
BF = jnp.bfloat16
F32 = jnp.float32
I32 = jnp.int32
MESH = pl.DeviceIdType.MESH


def up_to(value, step):
    return -(-value // step) * step


def layer_norm(values, gain_vec):
    values = values.astype(F32)
    center = jnp.mean(values, axis=-1, keepdims=True)
    offset_vals = values - center
    spread = jnp.mean(offset_vals * offset_vals, axis=-1, keepdims=True)
    return (offset_vals * lax.rsqrt(spread + epsilon) * gain_vec).astype(BF)


def dot32(left, right):
    return jnp.dot(left, right, preferred_element_type=F32)


def down(count):
    return lax.broadcasted_iota(I32, (count, 1), 0)


def along(count):
    return lax.broadcasted_iota(I32, (1, count), 1)


def one_hot(row_key, col_key):
    return (row_key == col_key).astype(F32).astype(BF)


def flat(block):
    return block.astype(F32).reshape(-1, block.shape[-1]).astype(BF)


def window_mask(limit):
    row = (lax.broadcasted_iota(I32, (WT, WT), 0) // WW) % WL
    col = (lax.broadcasted_iota(I32, (WT, WT), 1) // WW) % WL
    row_in = (row >= limit).astype(I32)
    col_in = (col >= limit).astype(I32)
    return jnp.where(row_in == col_in, 0.0, masked_score)


def head_order(heads, head_dim):
    lanes = heads * head_dim
    width = 3 * lanes
    row = down(width)
    col = along(width)
    origin = ((col % lanes) // head_dim) * (3 * head_dim) + (col // lanes) * head_dim + col % head_dim
    return one_hot(row, origin)


def attend(part, heads, head_dim, bias_at, place_mask):
    lanes = heads * head_dim
    queries = part[:, :lanes].astype(F32)
    keys_all = part[:, lanes : 2 * lanes].astype(BF)
    values = part[:, 2 * lanes :].astype(BF)
    lane = lax.broadcasted_iota(I32, (WT, lanes), 1) // head_dim
    total = None
    for h in range(heads):
        mine = jnp.where(lane == h, queries, 0.0).astype(BF)
        scores = lax.dot_general(
            mine, keys_all, (((1,), (1,)), ((), ())), preferred_element_type=F32
        )
        scores = scores * head_dim ** (-0.5) + bias_at(h) + place_mask
        top = jnp.max(scores, axis=-1, keepdims=True)
        lifted = jnp.exp(scores - top)
        weight_sum = jnp.sum(lifted, axis=-1, keepdims=True)
        mixed = dot32(lifted.astype(BF), values) / weight_sum
        mixed = jnp.where(lane == h, mixed, 0.0)
        total = mixed if total is None else total + mixed
    return total


class Copies:
    def __init__(self, send, recv, make):
        self.send, self.recv, self.make = send, recv, make

    def one(self, *index):
        src, dst, device = self.make(*index)
        return pltpu.make_async_remote_copy(
            src, dst, self.send.at[index], self.recv.at[index], device_id=device, device_id_type=MESH
        )


def step_kernel(cfg, names, *refs):
    r = dict(zip(names, refs))
    m, n, nz = cfg["m"], cfg["n"], cfg["n"] // 2
    pds, rows, cols = cfg["pds"], cfg["rows"], cfg["cols"]
    seg = WD * cols
    cells = rows * seg
    half = rows // 2
    hc = cols // 2
    per_row = WD * hc
    few = half * per_row
    fewp = up_to(few, 16)
    hal = up_to(HALO * per_row, 16)
    heads1, heads2, hd = cfg["heads1"], cfg["heads2"], cfg["hd"]
    lanes2 = heads2 * hd
    wins = rows // WL
    lat = lax.axis_index("lat")
    lon = lax.axis_index("lon")
    zi, core = lon // 2, lon % 2
    buddy = lon + 1 - 2 * core
    s0, s1, s2, s3 = r["off"][0], r["off"][1], r["off"][2], r["off"][3]

    def dev(dlat, dlon):
        return (lax.rem(lat + dlat + m, m), lax.rem(lon + dlon + n, n))

    greet = {(0, d) for d in range(1, n)}
    greet |= {(d % m, e) for d in (-1, 1) for e in range(n)}
    greet |= {(d, 0) for d in range(1, m)}
    greet -= {(0, 0)}
    barrier = pltpu.get_barrier_semaphore()
    for dlat, dlon in sorted(greet):
        pl.semaphore_signal(barrier, 1, device_id=dev(dlat, dlon), device_id_type=MESH)

    def local(k, src, dst):
        return pltpu.make_async_copy(src, dst, r["lsem"].at[k])

    E = [r["E%d" % pd] for pd in range(pds)]
    G = [r["G%d" % pd] for pd in range(pds)]
    loads = {
        "x0": local(0, r["x"].at[0], E[0].at[0, pl.ds(0, rows)]),
        "x1": local(1, r["x"].at[1], E[1].at[0, pl.ds(0, rows)]),
        "wt": local(2, r["wt"], r["v_wt"]),
        "b1": local(3, r["b1"], r["v_b1"]),
        "wo1": local(4, r["wo1"], r["v_wo1"]),
        "we1": local(5, r["we1"], r["v_we1"]),
        "wr1": local(6, r["wr1"], r["v_wr1"]),
        "mw": local(7, r["mw"], r["v_mw"]),
        "wt2": local(8, r["wt2"], r["v_wt2"].at[core]),
        "b2": local(9, r["b2"], r["v_b2"]),
        "we2": local(10, r["we2"], r["v_we2"].at[core]),
        "wr2": local(11, r["wr2"], r["v_wr2"].at[core]),
        "up": local(12, r["up"], r["v_up"]),
        "wo2": local(13, r["wo2"].at[lat], r["W"].at[core, lat, zi]),
    }
    for key in ("x0", "x1", "wt", "b1", "wo2"):
        loads[key].start()

    halo_copies = [
        Copies(r["hs%d" % k], r["hr%d" % k], make)
        for k, make in enumerate(
            (
                lambda pd: (r["x"].at[pd], E[pd].at[1, pl.ds(0, rows)], dev(0, -1)),
                lambda pd: (r["x"].at[pd, pl.ds(0, HALO)], E[pd].at[0, pl.ds(rows, HALO)], dev(-1, 0)),
                lambda pd: (r["x"].at[pd, pl.ds(0, HALO)], E[pd].at[1, pl.ds(rows, HALO)], dev(-1, -1)),
            )
        )
    ]
    low = rows - HALO
    back_copies = [
        Copies(r["bs%d" % k], r["br%d" % k], make)
        for k, make in enumerate(
            (
                lambda pd: (G[pd].at[0, pl.ds(HALO, rows)], G[pd].at[1, pl.ds(HALO, rows)], dev(0, 1)),
                lambda pd: (G[pd].at[0, pl.ds(HALO + low, HALO)], G[pd].at[0, pl.ds(0, HALO)], dev(1, 0)),
                lambda pd: (G[pd].at[0, pl.ds(HALO + low, HALO)], G[pd].at[1, pl.ds(0, HALO)], dev(1, 1)),
            )
        )
    ]
    W = r["W"]
    share_lon = Copies(
        r["ws0"], r["wr0"], lambda k: (r["wo2"].at[lat], W.at[core, lat, zi], dev(0, 2 * (k + 1)))
    )
    share_lat = Copies(r["ws1"], r["wr1s"], lambda k: (W.at[core, lat], W.at[core, lat], dev(k + 1, 0)))
    share_core = Copies(r["ws2"], r["wr2s"], lambda k: (W.at[core], W.at[core], (lat, buddy)))

    def swap(k):
        name = ("wt2", "we2", "wr2")[k]
        return pltpu.make_async_remote_copy(
            r[name],
            r["v_" + name].at[core],
            r["ss"].at[k],
            r["sr"].at[k],
            device_id=(lat, buddy),
            device_id_type=MESH,
        )

    X, Y, S, H = r["X"], r["Y"], r["S"], r["H"]
    gather1 = Copies(
        r["as0"], r["ar0"], lambda pd, k: (X.at[pd, zi], X.at[pd, zi], dev(0, 2 * (k + 1)))
    )
    cross = [
        Copies(r["cs%d" % k], r["cr%d" % k], make)
        for k, make in enumerate(
            (
                lambda pd: (S.at[pd], Y.at[pd, core], (lat, buddy)),
                lambda pd: (Y.at[pd, core, :, pl.ds(0, hal)], H.at[pd, core], dev(-1, 0)),
                lambda pd: (S.at[pd, :, pl.ds(0, hal)], H.at[pd, core], (lax.rem(lat + m - 1, m), buddy)),
            )
        )
    ]
    C, D, M, N = r["C"], r["D"], r["M"], r["N"]

    def to_owner(pd, k):
        owner = lax.rem(lon + k + 1, n)
        return C.at[pd, owner % 2, owner // 2, pl.ds(0, few)], M.at[pd, lon], (lat, owner)

    def to_next(pd, k):
        owner = lax.rem(lon + k, n)
        return D.at[pd, owner % 2, owner // 2], N.at[pd, lon], (lax.rem(lat + 1, m), owner)

    spread_here = Copies(r["ds0"], r["dr0"], to_owner)
    spread_next = Copies(r["ds1"], r["dr1"], to_next)
    Z, Q, T = r["Z"], r["Q"], r["T"]
    gather2 = Copies(
        r["as1"], r["ar1"], lambda pd, k: (Z.at[pd, zi], Z.at[pd, zi], dev(0, 2 * (k + 1)))
    )

    def partial_to(pd, k):
        peer = lax.rem(zi + k + 1, nz)
        return Q.at[pd, peer], T.at[pd, k], (lat, 2 * peer + core)

    scatter = Copies(r["rs0"], r["rr0"], partial_to)

    pl.semaphore_wait(barrier, len(greet))
    for pd in range(pds):
        for c in halo_copies:
            c.one(pd).start()
    for k in range(nz - 1):
        share_lon.one(k).start()
    for k in range(3):
        swap(k).start()
    for key in ("wo1", "we1", "wr1", "mw", "wt2", "b2", "we2", "wr2", "up"):
        loads[key].start()

    def place(index):
        return index // (WL * WW), (index // WW) % WL, index % WW

    a, b, c = place(down(WT))
    q = along(2 * WL * seg)
    r["P1"][...] = one_hot(
        (b * WD + a) * 64 + c + s1,
        ((q % (WL * seg)) // cols) * 64 + (q // (WL * seg)) * cols + q % cols,
    )
    a, b, c = place(along(WT))
    row = down(WT)
    r["U1"][...] = one_hot(row, (b * WD + a) * WW + c)

    def blocked(index):
        block, cell = index // few, index % few
        i = (cell // per_row) * 2 + block % 2
        j = (cell % hc) * 2 + block // 2
        return i * WD + (cell // hc) % WD, j

    ia, j = blocked(down(cells))
    q = along(2 * cells)
    r["B1"][...] = one_hot(
        ia * 64 + j - s1 + cols,
        ((q % cells) // cols) * 64 + jnp.where(q < cells, cols, 0) + q % cols,
    )
    q = along(cells)
    r["B0"][...] = one_hot(ia * cols + j, q)
    ia, j = blocked(along(cells))
    r["B2"][...] = one_hot(down(cells), ia * cols + j)

    def own_key(index, size, first):
        return jnp.where(
            index < size, (index // hc + first * WD) * 64 + index % hc, -1
        )

    a, b, c = place(down(WT))
    q = along(4 * fewp + 4 * hal)
    far = q >= 4 * fewp
    qh = q - 4 * fewp
    chunk = jnp.where(far, qh // hal, q // fewp)
    key = jnp.where(far, own_key(qh % hal, HALO * per_row, half), own_key(q % fewp, few, 0))
    r["P2"][...] = one_hot(
        ((b + s2) * WD + a) * 64 + c + s3, jnp.where(key < 0, -1, key + chunk * hc)
    )
    a, b, c = place(along(2 * WT) % WT)
    x = c + s3 - jnp.where(along(2 * WT) < WT, 0, cols)
    col_key = jnp.where((x >= 0) & (x < cols), ((b + s2) * WD + a) * 64 + x, -2)
    q = down(2 * fewp + 2 * hal)
    far = q >= 2 * fewp
    qh = q - 2 * fewp
    chunk = jnp.where(far, qh // hal, q // fewp)
    key = jnp.where(far, own_key(qh % hal, HALO * per_row, half), own_key(q % fewp, few, 0))
    r["U2"][...] = one_hot(jnp.where(key < 0, -1, key + chunk * hc), col_key)

    pad = jnp.zeros((fewp - few, 3 * lanes2), BF)
    for pd in range(pds):
        for z in range(nz):
            S[pd, z, few:] = pad
    for k in range(wins):
        r["K1"][k] = window_mask(rows * m - s0 - lat * rows - k * WL)
    r["K2"][...] = window_mask(half * m - s2 - lat * half)

    group = 4 if heads1 % 4 == 0 else heads1
    width = 3 * group * hd
    loads["wt"].wait()
    order = head_order(group, hd)
    for g in range(heads1 // group):
        cut = slice(g * width, (g + 1) * width)
        r["wt_o"][:, cut] = dot32(r["v_wt"][:, cut], order).astype(BF)
    loads["x0"].wait()
    loads["x1"].wait()
    for pd in range(pds):
        r["F"][pd] = dot32(r["B0"][...], flat(E[pd][0, :rows])).astype(BF)
    loads["b1"].wait()

    def fine_attention(pd):
        for cps in halo_copies:
            cps.one(pd).wait_recv()
        for k in range(wins):
            near = flat(E[pd][:, pl.ds(s0 + k * WL, WL)])
            framed = dot32(r["P1"][...], near)
            r["A"][pl.ds(k * WT, WT), :] = layer_norm(framed, r["g1"][...])
        r["tri"][...] = dot32(r["A"][...], r["wt_o"][...]).astype(BF)

        def one_group(g, carry):
            for k in range(wins):
                part = r["tri"][pl.ds(k * WT, WT), pl.ds(pl.multiple_of(g * width, 128), width)]
                total = attend(part, group, hd, lambda h: r["v_b1"][g * group + h], r["K1"][k])
                r["A"][pl.ds(k * WT, WT), pl.ds(pl.multiple_of(g * group * hd, 128), group * hd)] = (
                    total.astype(BF)
                )
            return carry

        lax.fori_loop(0, heads1 // group, one_group, 0)
        for k in range(wins):
            turned = dot32(r["U1"][...], r["A"][pl.ds(k * WT, WT), :])
            G[pd][0, pl.ds(HALO + k * WL, WL)] = turned.reshape(WL, seg, -1).astype(BF)
        for cps in back_copies:
            cps.one(pd).start()

    for pd in range(pds):
        fine_attention(pd)

    for k in range(nz - 1):
        share_lon.one(k).wait_recv()
    loads["wo2"].wait()
    for k in range(m - 1):
        share_lat.one(k).start()
    for key in ("wo1", "we1", "wr1", "mw"):
        loads[key].wait()

    def fine_tail(pd):
        for cps in back_copies:
            cps.one(pd).wait_recv()
        r["near"][...] = flat(G[pd][:, pl.ds(HALO - s0, rows)])

        def some_rows(k, carry):
            at = pl.ds(pl.multiple_of(k * (cells // 2), 16), cells // 2)
            mixed = dot32(r["B1"][at, :], r["near"][...]).astype(BF)
            attended = (r["F"][pd, at, :].astype(F32) + dot32(mixed, r["v_wo1"][...])).astype(BF)
            normed = layer_norm(attended, r["gm"][...])
            hidden = jax.nn.gelu(dot32(normed, r["v_we1"][...])).astype(BF)
            state = (attended.astype(F32) + dot32(hidden, r["v_wr1"][...])).astype(BF)
            r["state"][pd, at, :] = state.astype(F32)
            return carry

        lax.fori_loop(0, 2, some_rows, 0)
        merged = jnp.concatenate([r["state"][pd, k * few : (k + 1) * few, :] for k in range(4)], axis=1)
        coarse_in = dot32(layer_norm(merged, r["mg"][...]), r["v_mw"][...]).astype(BF)
        r["cin"][pd] = coarse_in
        X[pd, zi] = layer_norm(coarse_in, r["g2"][...])
        for k in range(nz - 1):
            gather1.one(pd, k).start()

    for pd in range(pds):
        fine_tail(pd)

    for k in range(m - 1):
        share_lat.one(k).wait_recv()
    share_core.one(0).start()
    loads["wt2"].wait()
    swap(0).wait_recv()
    order = head_order(heads2, hd)
    for k in range(2):
        r["wt2_o"][k] = dot32(r["v_wt2"][k], order).astype(BF)

    def coarse_project(pd, carry):
        for k in range(nz - 1):
            gather1.one(pd, k).wait_recv()
        given = flat(X[pd])
        theirs = dot32(given, r["wt2_o"][1 - core]).reshape(nz, few, -1).astype(BF)
        S[pd, :, pl.ds(0, few)] = theirs
        cross[0].one(pd).start()
        cross[2].one(pd).start()
        mine = dot32(given, r["wt2_o"][core]).reshape(nz, few, -1).astype(BF)
        Y[pd, core, :, pl.ds(0, few)] = mine
        for z in range(nz):
            Y[pd, core, z, few:] = pad
        cross[1].one(pd).start()
        return carry

    lax.fori_loop(0, pds, coarse_project, 0)
    loads["b2"].wait()

    def coarse_attention(pd, carry):
        for cps in cross:
            cps.one(pd).wait_recv()

        def one_window(w, carry):
            zs = [lax.rem(w + dz, nz) for dz in range(2)]
            pieces = [Y[pd, par, z] for z in zs for par in range(2)]
            pieces += [H[pd, par, z] for z in zs for par in range(2)]
            part = dot32(r["P2"][...], jnp.concatenate(pieces, axis=0))
            total = attend(part, heads2, hd, lambda h: r["v_b2"][h], r["K2"][...])
            r["V"][w] = total.astype(BF)
            return carry

        lax.fori_loop(0, nz, one_window, 0)

        def one_chip(z, carry):
            both = jnp.concatenate([r["V"][z], r["V"][lax.rem(z + nz - 1, nz)]], axis=0)
            back = dot32(r["U2"][...], both).astype(BF)
            for par in range(2):
                C[pd, par, z] = back[par * fewp : (par + 1) * fewp]
                D[pd, par, z] = back[2 * fewp + par * hal : 2 * fewp + (par + 1) * hal]
            return carry

        lax.fori_loop(0, nz, one_chip, 0)
        for k in range(n - 1):
            spread_here.one(pd, k).start()
        for k in range(n):
            spread_next.one(pd, k).start()
        M[pd, lon] = C[pd, core, zi, pl.ds(0, few)]
        return carry

    lax.fori_loop(0, pds, coarse_attention, 0)
    share_core.one(0).wait_recv()

    def coarse_output(pd, carry):
        for k in range(n - 1):
            spread_here.one(pd, k).wait_recv()
        for k in range(n):
            spread_next.one(pd, k).wait_recv()
        value = r["cin"][pd].astype(F32)
        tail = jnp.zeros((few - hal, lanes2), F32)
        for g in range(n):
            part = M[pd, g].astype(F32) + jnp.concatenate([N[pd, g].astype(F32), tail], axis=0)
            value += dot32(part.astype(BF), flat(W[g % 2, :, g // 2]))
        middle = value.astype(BF)
        r["mid"][pd] = middle
        Z[pd, zi] = layer_norm(middle, r["gm2"][...])
        for k in range(nz - 1):
            gather2.one(pd, k).start()
        return carry

    lax.fori_loop(0, pds, coarse_output, 0)
    for key in ("we2", "wr2", "up"):
        loads[key].wait()
    swap(1).wait_recv()
    swap(2).wait_recv()

    def coarse_feed(pd, carry):
        for k in range(nz - 1):
            gather2.one(pd, k).wait_recv()
        given = flat(Z[pd])
        total = None
        for k in range(2):
            hidden = jax.nn.gelu(dot32(given, r["v_we2"][k])).astype(BF)
            term = dot32(hidden, r["v_wr2"][k])
            total = term if total is None else total + term
        total = total.reshape(nz, few, -1)
        r["sum"][...] = total
        Q[pd] = total.astype(BF)
        r["own"][pd] = r["sum"][zi]
        for k in range(nz - 1):
            scatter.one(pd, k).start()
        return carry

    lax.fori_loop(0, pds, coarse_feed, 0)

    def finish(pd, carry):
        for k in range(nz - 1):
            scatter.one(pd, k).wait_recv()
        value = r["mid"][pd].astype(F32) + r["own"][pd]
        for k in range(nz - 1):
            value += T[pd, k].astype(F32)
        state = value.astype(BF)
        r["cstate"][pd] = state
        expanded = dot32(state, r["v_up"][...])
        channels = expanded.shape[1] // 4
        for k in range(4):
            at = slice(k * few, (k + 1) * few)
            cut = slice(k * channels, (k + 1) * channels)
            r["state"][pd, at, :] = r["state"][pd, at, :] + expanded[:, cut]
        r["blended"][pd] = dot32(r["B2"][...], r["state"][pd].astype(BF)).astype(BF)
        return carry

    lax.fori_loop(0, pds, finish, 0)

    for pd in range(pds):
        for cps in halo_copies + back_copies + cross:
            cps.one(pd).wait_send()
        for k in range(nz - 1):
            for cps in (gather1, gather2, scatter):
                cps.one(pd, k).wait_send()
        for k in range(n - 1):
            spread_here.one(pd, k).wait_send()
        for k in range(n):
            spread_next.one(pd, k).wait_send()
    for k in range(nz - 1):
        share_lon.one(k).wait_send()
    for k in range(m - 1):
        share_lat.one(k).wait_send()
    share_core.one(0).wait_send()
    for k in range(3):
        swap(k).wait_send()


def body(
    fine_field,
    offsets,
    fine_prenorm,
    fine_triple,
    fine_bias,
    fine_output,
    fine_midnorm,
    fine_expand,
    fine_reduce,
    merge_gain,
    merge_weight,
    coarse_prenorm,
    coarse_triple,
    coarse_bias,
    coarse_output,
    coarse_midnorm,
    coarse_expand,
    coarse_reduce,
    upsample_weight,
):
    levels, rows, cols, channels = fine_field.shape
    m = lax.axis_size("lat")
    n = lax.axis_size("lon")
    nz = n // 2
    pds = levels // WD
    wide = coarse_output.shape[1]
    heads1, heads2 = fine_bias.shape[0], coarse_bias.shape[0]
    hd = channels // heads1
    lanes2 = coarse_output.shape[0]
    assert cols == WW and rows == 2 * WL and n % 2 == 0 and nz >= 2 and pds == 2
    assert lanes2 == heads2 * hd and lanes2 % m == 0
    half, hc = rows // 2, cols // 2
    seg = WD * cols
    cells = rows * seg
    few = cells // 4
    fewp = up_to(few, 16)
    hal = up_to(HALO * WD * hc, 16)

    x = fine_field.reshape(pds, WD, rows, cols, channels).transpose(0, 2, 1, 3, 4)
    x = x.reshape(pds, rows, seg, channels)
    vmem = pl.BlockSpec(memory_space=pltpu.VMEM)
    hbm = pl.BlockSpec(memory_space=pl.ANY)
    args = [
        ("off", offsets, pl.BlockSpec(memory_space=pltpu.SMEM)),
        ("x", x, hbm),
        ("g1", fine_prenorm[None], vmem),
        ("wt", fine_triple, hbm),
        ("b1", fine_bias, hbm),
        ("wo1", fine_output, hbm),
        ("gm", fine_midnorm[None], vmem),
        ("we1", fine_expand, hbm),
        ("wr1", fine_reduce, hbm),
        ("mg", merge_gain[None], vmem),
        ("mw", merge_weight, hbm),
        ("g2", coarse_prenorm[None], vmem),
        ("wt2", coarse_triple, hbm),
        ("b2", coarse_bias, hbm),
        ("wo2", coarse_output.reshape(m, lanes2 // m, wide), hbm),
        ("gm2", coarse_midnorm[None], vmem),
        ("we2", coarse_expand, hbm),
        ("wr2", coarse_reduce, hbm),
        ("up", upsample_weight, hbm),
    ]
    outs = [
        ("blended", jax.ShapeDtypeStruct((pds, cells, channels), BF)),
        ("cstate", jax.ShapeDtypeStruct((pds, few, wide), BF)),
    ]
    sem = pltpu.SemaphoreType.DMA
    wide3 = 3 * lanes2
    scratch = [
        ("lsem", sem((14,))),
        ("v_wt", pltpu.VMEM(fine_triple.shape, BF)),
        ("wt_o", pltpu.VMEM(fine_triple.shape, BF)),
        ("v_b1", pltpu.VMEM(fine_bias.shape, F32)),
        ("v_wo1", pltpu.VMEM(fine_output.shape, BF)),
        ("v_we1", pltpu.VMEM(fine_expand.shape, BF)),
        ("v_wr1", pltpu.VMEM(fine_reduce.shape, BF)),
        ("v_mw", pltpu.VMEM(merge_weight.shape, BF)),
        ("v_wt2", pltpu.VMEM((2,) + coarse_triple.shape, BF)),
        ("wt2_o", pltpu.VMEM((2,) + coarse_triple.shape, BF)),
        ("v_b2", pltpu.VMEM(coarse_bias.shape, F32)),
        ("v_we2", pltpu.VMEM((2,) + coarse_expand.shape, BF)),
        ("v_wr2", pltpu.VMEM((2,) + coarse_reduce.shape, BF)),
        ("v_up", pltpu.VMEM(upsample_weight.shape, BF)),
        ("W", pltpu.VMEM((2, m, nz, lanes2 // m, wide), BF)),
        ("P1", pltpu.VMEM((WT, 2 * WL * seg), BF)),
        ("U1", pltpu.VMEM((WT, WT), BF)),
        ("B0", pltpu.VMEM((cells, cells), BF)),
        ("B1", pltpu.VMEM((cells, 2 * cells), BF)),
        ("B2", pltpu.VMEM((cells, cells), BF)),
        ("P2", pltpu.VMEM((WT, 4 * fewp + 4 * hal), BF)),
        ("U2", pltpu.VMEM((2 * fewp + 2 * hal, 2 * WT), BF)),
        ("K1", pltpu.VMEM((rows // WL, WT, WT), F32)),
        ("K2", pltpu.VMEM((WT, WT), F32)),
        ("F", pltpu.VMEM((pds, cells, channels), BF)),
        ("A", pltpu.VMEM((cells, channels), BF)),
        ("tri", pltpu.VMEM((cells, 3 * channels), BF)),
        ("near", pltpu.VMEM((2 * cells, channels), BF)),
        ("state", pltpu.VMEM((pds, cells, channels), F32)),
        ("cin", pltpu.VMEM((pds, few, wide), BF)),
        ("X", pltpu.VMEM((pds, nz, few, wide), BF)),
        ("Y", pltpu.VMEM((pds, 2, nz, fewp, wide3), BF)),
        ("S", pltpu.VMEM((pds, nz, fewp, wide3), BF)),
        ("H", pltpu.VMEM((pds, 2, nz, hal, wide3), BF)),
        ("V", pltpu.VMEM((nz, WT, lanes2), BF)),
        ("C", pltpu.VMEM((pds, 2, nz, fewp, lanes2), BF)),
        ("D", pltpu.VMEM((pds, 2, nz, hal, lanes2), BF)),
        ("M", pltpu.VMEM((pds, n, few, lanes2), BF)),
        ("N", pltpu.VMEM((pds, n, hal, lanes2), BF)),
        ("mid", pltpu.VMEM((pds, few, wide), BF)),
        ("Z", pltpu.VMEM((pds, nz, few, wide), BF)),
        ("sum", pltpu.VMEM((nz, few, wide), F32)),
        ("own", pltpu.VMEM((pds, few, wide), F32)),
        ("Q", pltpu.VMEM((pds, nz, few, wide), BF)),
        ("T", pltpu.VMEM((pds, nz - 1, few, wide), BF)),
    ]
    for pd in range(pds):
        for name in ("E", "G"):
            scratch.append((name + str(pd), pltpu.VMEM((2, rows + HALO, seg, channels), BF)))
    for name in ("h", "b", "c"):
        for k in range(3):
            scratch += [("%ss%d" % (name, k), sem((pds,))), ("%sr%d" % (name, k), sem((pds,)))]
    for s, d, shape in (
        ("ws0", "wr0", (nz - 1,)),
        ("ws1", "wr1s", (m - 1,)),
        ("ws2", "wr2s", (1,)),
        ("ss", "sr", (3,)),
        ("as0", "ar0", (pds, nz - 1)),
        ("as1", "ar1", (pds, nz - 1)),
        ("ds0", "dr0", (pds, n - 1)),
        ("ds1", "dr1", (pds, n)),
        ("rs0", "rr0", (pds, nz - 1)),
    ):
        scratch += [(s, sem(shape)), (d, sem(shape))]

    cfg = dict(m=m, n=n, pds=pds, rows=rows, cols=cols, heads1=heads1, heads2=heads2, hd=hd)
    names = [a[0] for a in args] + [o[0] for o in outs] + [s[0] for s in scratch]
    blended, state = pl.pallas_call(
        functools.partial(step_kernel, cfg, names),
        out_shape=[o[1] for o in outs],
        in_specs=[a[2] for a in args],
        out_specs=[vmem, vmem],
        scratch_shapes=[s[1] for s in scratch],
        compiler_params=pltpu.CompilerParams(
            collective_id=0, has_side_effects=True, vmem_limit_bytes=63 << 20
        ),
    )(*[a[1] for a in args])
    blended = blended.reshape(pds, rows, WD, cols, channels).transpose(0, 2, 1, 3, 4)
    state = state.reshape(pds, half, WD, hc, wide).transpose(0, 2, 1, 3, 4)
    return (
        blended.reshape(levels, rows, cols, channels),
        state.reshape(levels, half, hc, wide),
    )


def solution(mesh):
    placed = (
        P(None, "lat", "lon", None),
        P(),
        P(),
        P(),
        P(),
        P(),
        P(),
        P(),
        P(),
        P(),
        P(),
        P(),
        P(None, "lon"),
        P("lon", None, None),
        P("lon", None),
        P(),
        P(None, "lon"),
        P("lon", None),
        P(),
    )
    return jax.shard_map(
        body,
        mesh=mesh,
        in_specs=placed,
        out_specs=(P(None, "lat", "lon", None), P(None, "lat", "lon", None)),
        check_vma=False,
    )
```

```python
import functools

import jax
import jax.numpy as jnp
from jax import lax
from jax.experimental import pallas as pl
from jax.experimental.pallas import tpu as pltpu
from jax.sharding import PartitionSpec as P

WD = 2
WL = 6
WW = 12
WT = 144
HALO = WL - 1

epsilon = 1e-05
masked_score = -1e30
BF = jnp.bfloat16
F32 = jnp.float32
I32 = jnp.int32
MESH = pl.DeviceIdType.MESH


def up_to(value, step):
    return -(-value // step) * step


def layer_norm(values, gain_vec):
    values = values.astype(F32)
    center = jnp.mean(values, axis=-1, keepdims=True)
    offset_vals = values - center
    spread = jnp.mean(offset_vals * offset_vals, axis=-1, keepdims=True)
    return (offset_vals * lax.rsqrt(spread + epsilon) * gain_vec).astype(BF)


def dot32(left, right):
    return jnp.dot(left, right, preferred_element_type=F32)


def down(count):
    return lax.broadcasted_iota(I32, (count, 1), 0)


def along(count):
    return lax.broadcasted_iota(I32, (1, count), 1)


def one_hot(row_key, col_key):
    return (row_key == col_key).astype(F32).astype(BF)


def flat(block):
    return block.astype(F32).reshape(-1, block.shape[-1]).astype(BF)


def window_mask(limit):
    row = (lax.broadcasted_iota(I32, (WT, WT), 0) // WW) % WL
    col = (lax.broadcasted_iota(I32, (WT, WT), 1) // WW) % WL
    row_in = (row >= limit).astype(I32)
    col_in = (col >= limit).astype(I32)
    return jnp.where(row_in == col_in, 0.0, masked_score)


def head_order(heads, head_dim):
    lanes = heads * head_dim
    width = 3 * lanes
    row = down(width)
    col = along(width)
    origin = ((col % lanes) // head_dim) * (3 * head_dim) + (col // lanes) * head_dim + col % head_dim
    return one_hot(row, origin)


def attend(part, heads, head_dim, bias_at, place_mask):
    lanes = heads * head_dim
    queries = part[:, :lanes].astype(F32)
    keys_all = part[:, lanes : 2 * lanes].astype(BF)
    values = part[:, 2 * lanes :].astype(BF)
    lane = lax.broadcasted_iota(I32, (WT, lanes), 1) // head_dim
    total = None
    for h in range(heads):
        mine = jnp.where(lane == h, queries, 0.0).astype(BF)
        scores = lax.dot_general(
            mine, keys_all, (((1,), (1,)), ((), ())), preferred_element_type=F32
        )
        scores = scores * head_dim ** (-0.5) + bias_at(h) + place_mask
        top = jnp.max(scores, axis=-1, keepdims=True)
        lifted = jnp.exp(scores - top)
        weight_sum = jnp.sum(lifted, axis=-1, keepdims=True)
        mixed = dot32(lifted.astype(BF), values) / weight_sum
        mixed = jnp.where(lane == h, mixed, 0.0)
        total = mixed if total is None else total + mixed
    return total


class Copies:
    def __init__(self, send, recv, make):
        self.send, self.recv, self.make = send, recv, make

    def one(self, *index):
        src, dst, device = self.make(*index)
        return pltpu.make_async_remote_copy(
            src, dst, self.send.at[index], self.recv.at[index], device_id=device, device_id_type=MESH
        )


def step_kernel(cfg, names, *refs):
    r = dict(zip(names, refs))
    m, n, nz = cfg["m"], cfg["n"], cfg["n"] // 2
    pds, rows, cols = cfg["pds"], cfg["rows"], cfg["cols"]
    seg = WD * cols
    cells = rows * seg
    half = rows // 2
    hc = cols // 2
    per_row = WD * hc
    few = half * per_row
    fewp = up_to(few, 16)
    hal = up_to(HALO * per_row, 16)
    heads1, heads2, hd = cfg["heads1"], cfg["heads2"], cfg["hd"]
    lanes2 = heads2 * hd
    wins = rows // WL
    lat = lax.axis_index("lat")
    lon = lax.axis_index("lon")
    zi, core = lon // 2, lon % 2
    buddy = lon + 1 - 2 * core
    s0, s1, s2, s3 = r["off"][0], r["off"][1], r["off"][2], r["off"][3]

    def dev(dlat, dlon):
        return (lax.rem(lat + dlat + m, m), lax.rem(lon + dlon + n, n))

    greet = {(0, d) for d in range(1, n)}
    greet |= {(d % m, e) for d in (-1, 1) for e in range(n)}
    greet |= {(d, 0) for d in range(1, m)}
    greet -= {(0, 0)}
    barrier = pltpu.get_barrier_semaphore()
    for dlat, dlon in sorted(greet):
        pl.semaphore_signal(barrier, 1, device_id=dev(dlat, dlon), device_id_type=MESH)

    def local(k, src, dst):
        return pltpu.make_async_copy(src, dst, r["lsem"].at[k])

    E = [r["E%d" % pd] for pd in range(pds)]
    G = [r["G%d" % pd] for pd in range(pds)]
    loads = {
        "x0": local(0, r["x"].at[0], E[0].at[0, pl.ds(0, rows)]),
        "x1": local(1, r["x"].at[1], E[1].at[0, pl.ds(0, rows)]),
        "wt": local(2, r["wt"], r["v_wt"]),
        "b1": local(3, r["b1"], r["v_b1"]),
        "wo1": local(4, r["wo1"], r["v_wo1"]),
        "we1": local(5, r["we1"], r["v_we1"]),
        "wr1": local(6, r["wr1"], r["v_wr1"]),
        "mw": local(7, r["mw"], r["v_mw"]),
        "wt2": local(8, r["wt2"], r["v_wt2"].at[core]),
        "b2": local(9, r["b2"], r["v_b2"]),
        "we2": local(10, r["we2"], r["v_we2"].at[core]),
        "wr2": local(11, r["wr2"], r["v_wr2"].at[core]),
        "up": local(12, r["up"], r["v_up"]),
        "wo2": local(13, r["wo2"].at[lat], r["W"].at[core, lat, zi]),
    }
    for key in ("x0", "x1", "wt", "b1", "wo2"):
        loads[key].start()

    halo_copies = [
        Copies(r["hs%d" % k], r["hr%d" % k], make)
        for k, make in enumerate(
            (
                lambda pd: (r["x"].at[pd], E[pd].at[1, pl.ds(0, rows)], dev(0, -1)),
                lambda pd: (r["x"].at[pd, pl.ds(0, HALO)], E[pd].at[0, pl.ds(rows, HALO)], dev(-1, 0)),
                lambda pd: (r["x"].at[pd, pl.ds(0, HALO)], E[pd].at[1, pl.ds(rows, HALO)], dev(-1, -1)),
            )
        )
    ]
    low = rows - HALO
    back_copies = [
        Copies(r["bs%d" % k], r["br%d" % k], make)
        for k, make in enumerate(
            (
                lambda pd: (G[pd].at[0, pl.ds(HALO, rows)], G[pd].at[1, pl.ds(HALO, rows)], dev(0, 1)),
                lambda pd: (G[pd].at[0, pl.ds(HALO + low, HALO)], G[pd].at[0, pl.ds(0, HALO)], dev(1, 0)),
                lambda pd: (G[pd].at[0, pl.ds(HALO + low, HALO)], G[pd].at[1, pl.ds(0, HALO)], dev(1, 1)),
            )
        )
    ]
    W = r["W"]
    share_lon = Copies(
        r["ws0"], r["wr0"], lambda k: (W.at[core, lat, zi], W.at[core, lat, zi], dev(0, 2 * (k + 1)))
    )
    share_lat = Copies(r["ws1"], r["wr1s"], lambda k: (W.at[core, lat], W.at[core, lat], dev(k + 1, 0)))
    share_core = Copies(r["ws2"], r["wr2s"], lambda k: (W.at[core], W.at[core], (lat, buddy)))

    def swap(k):
        name = ("wt2", "we2", "wr2")[k]
        return pltpu.make_async_remote_copy(
            r[name],
            r["v_" + name].at[core],
            r["ss"].at[k],
            r["sr"].at[k],
            device_id=(lat, buddy),
            device_id_type=MESH,
        )

    X, Y, S, H = r["X"], r["Y"], r["S"], r["H"]

    def relay(buf, sends, recvs):
        def hop(pd, z, way, reach):
            step = 2 - 4 * way
            return pltpu.make_async_remote_copy(
                buf.at[pd, z],
                buf.at[pd, z],
                r[sends].at[pd, way, reach - 1],
                r[recvs].at[pd, way, reach - 1],
                device_id=(lat, lon + step),
                device_id_type=MESH,
            )

        def pass_on(pd, z, way, reach, act):
            @pl.when(jnp.where(way == 0, zi < nz - 1, zi > 0))
            def _():
                act(hop(pd, z, way, reach))

        def start(pd):
            for way in range(2):
                pass_on(pd, zi, way, 1, lambda c: c.start())

        def turn(j):
            both = jnp.minimum(zi, nz - 1 - zi)
            even = j < 2 * both
            way = jnp.where(even, j % 2, jnp.where(zi > nz - 1 - zi, 0, 1))
            reach = jnp.where(even, j // 2 + 1, j - both + 1)
            return zi - reach * (1 - 2 * way), way, reach

        def arrive(pd, j):
            z, way, reach = turn(j)
            hop(pd, z, way, reach).wait_recv()

            @pl.when(reach < nz - 1)
            def _():
                pass_on(pd, z, way, reach + 1, lambda c: c.start())

            return z

        def drain(pd):
            def one(j, carry):
                z, way, reach = turn(j)

                @pl.when(reach < nz - 1)
                def _():
                    pass_on(pd, z, way, reach + 1, lambda c: c.wait_send())

                return carry

            for way in range(2):
                pass_on(pd, zi, way, 1, lambda c: c.wait_send())
            lax.fori_loop(0, nz - 1, one, 0)

        return start, arrive, drain

    gather1_start, gather1_arrive, gather1_drain = relay(X, "as0", "ar0")
    cross = [
        Copies(r["cs%d" % k], r["cr%d" % k], make)
        for k, make in enumerate(
            (
                lambda pd, z: (S.at[pd, z], Y.at[pd, core, z], (lat, buddy)),
                lambda pd, z: (Y.at[pd, core, z, pl.ds(0, hal)], H.at[pd, core, z], dev(-1, 0)),
                lambda pd, z: (S.at[pd, z, pl.ds(0, hal)], H.at[pd, core, z], (lax.rem(lat + m - 1, m), buddy)),
            )
        )
    ]
    C, D, M, N = r["C"], r["D"], r["M"], r["N"]

    def to_owner(pd, k):
        owner = lax.rem(lon + k + 1, n)
        return C.at[pd, owner % 2, owner // 2, pl.ds(0, few)], M.at[pd, lon], (lat, owner)

    def to_next(pd, k):
        owner = lax.rem(lon + k, n)
        return D.at[pd, owner % 2, owner // 2], N.at[pd, lon], (lax.rem(lat + 1, m), owner)

    spread_here = Copies(r["ds0"], r["dr0"], to_owner)
    spread_next = Copies(r["ds1"], r["dr1"], to_next)
    Z, Q, T = r["Z"], r["Q"], r["T"]
    gather2_start, gather2_arrive, gather2_drain = relay(Z, "as1", "ar1")

    def partial_to(pd, z):
        return pltpu.make_async_remote_copy(
            Q.at[pd, z],
            T.at[pd, zi],
            r["rs0"].at[pd, z],
            r["rr0"].at[pd, zi],
            device_id=(lat, 2 * z + core),
            device_id_type=MESH,
        )

    def partial_from(pd, z):
        return pltpu.make_async_remote_copy(
            Q.at[pd, z],
            T.at[pd, z],
            r["rs0"].at[pd, z],
            r["rr0"].at[pd, z],
            device_id=(lat, 2 * z + core),
            device_id_type=MESH,
        )


    def place(index):
        return index // (WL * WW), (index // WW) % WL, index % WW

    a, b, c = place(down(WT))
    q = along(2 * WL * seg)
    r["P1"][...] = one_hot(
        (b * WD + a) * 64 + c + s1,
        ((q % (WL * seg)) // cols) * 64 + (q // (WL * seg)) * cols + q % cols,
    )
    a, b, c = place(along(WT))
    row = down(WT)
    r["U1"][...] = one_hot(row, (b * WD + a) * WW + c)

    def blocked(index):
        block, cell = index // few, index % few
        i = (cell // per_row) * 2 + block % 2
        j = (cell % hc) * 2 + block // 2
        return i * WD + (cell // hc) % WD, j

    ia, j = blocked(down(cells))
    q = along(2 * cells)
    r["B1"][...] = one_hot(
        ia * 64 + j - s1 + cols,
        ((q % cells) // cols) * 64 + jnp.where(q < cells, cols, 0) + q % cols,
    )
    q = along(cells)
    r["B0"][...] = one_hot(ia * cols + j, q)
    ia, j = blocked(along(cells))
    r["B2"][...] = one_hot(down(cells), ia * cols + j)

    def own_key(index, size, first):
        return jnp.where(
            index < size, (index // hc + first * WD) * 64 + index % hc, -1
        )

    a, b, c = place(down(WT))
    q = along(4 * fewp + 4 * hal)
    far = q >= 4 * fewp
    qh = q - 4 * fewp
    chunk = jnp.where(far, qh // hal, q // fewp)
    key = jnp.where(far, own_key(qh % hal, HALO * per_row, half), own_key(q % fewp, few, 0))
    r["P2"][...] = one_hot(
        ((b + s2) * WD + a) * 64 + c + s3, jnp.where(key < 0, -1, key + chunk * hc)
    )
    a, b, c = place(along(2 * WT) % WT)
    x = c + s3 - jnp.where(along(2 * WT) < WT, 0, cols)
    col_key = jnp.where((x >= 0) & (x < cols), ((b + s2) * WD + a) * 64 + x, -2)
    q = down(2 * fewp + 2 * hal)
    far = q >= 2 * fewp
    qh = q - 2 * fewp
    chunk = jnp.where(far, qh // hal, q // fewp)
    key = jnp.where(far, own_key(qh % hal, HALO * per_row, half), own_key(q % fewp, few, 0))
    r["U2"][...] = one_hot(jnp.where(key < 0, -1, key + chunk * hc), col_key)

    pad = jnp.zeros((fewp - few, 3 * lanes2), BF)
    for pd in range(pds):
        for z in range(nz):
            S[pd, z, few:] = pad
    for k in range(wins):
        r["K1"][k] = window_mask(rows * m - s0 - lat * rows - k * WL)
    r["K2"][...] = window_mask(half * m - s2 - lat * half)

    pl.semaphore_wait(barrier, len(greet))
    for pd in range(pds):
        for cps in halo_copies:
            cps.one(pd).start()
    loads["wo2"].wait()
    for k in range(nz - 1):
        share_lon.one(k).start()
    for k in range(3):
        swap(k).start()
    for key in ("we2", "wr2", "wt2", "wo1", "we1", "wr1", "mw", "b2", "up"):
        loads[key].start()

    group = 4 if heads1 % 4 == 0 else heads1
    width = 3 * group * hd
    loads["wt"].wait()
    order = head_order(group, hd)
    for g in range(heads1 // group):
        cut = slice(g * width, (g + 1) * width)
        r["wt_o"][:, cut] = dot32(r["v_wt"][:, cut], order).astype(BF)
    loads["x0"].wait()
    loads["x1"].wait()
    for pd in range(pds):
        r["F"][pd] = dot32(r["B0"][...], flat(E[pd][0, :rows])).astype(BF)
    loads["b1"].wait()

    def fine_attention(pd):
        for cps in halo_copies:
            cps.one(pd).wait_recv()
        for k in range(wins):
            near = flat(E[pd][:, pl.ds(s0 + k * WL, WL)])
            framed = dot32(r["P1"][...], near)
            r["A"][pl.ds(k * WT, WT), :] = layer_norm(framed, r["g1"][...])
        r["tri"][...] = dot32(r["A"][...], r["wt_o"][...]).astype(BF)

        def one_group(g, carry):
            for k in range(wins):
                part = r["tri"][pl.ds(k * WT, WT), pl.ds(pl.multiple_of(g * width, 128), width)]
                total = attend(part, group, hd, lambda h: r["v_b1"][g * group + h], r["K1"][k])
                r["A"][pl.ds(k * WT, WT), pl.ds(pl.multiple_of(g * group * hd, 128), group * hd)] = (
                    total.astype(BF)
                )
            return carry

        lax.fori_loop(0, heads1 // group, one_group, 0)
        for k in range(wins):
            turned = dot32(r["U1"][...], r["A"][pl.ds(k * WT, WT), :])
            G[pd][0, pl.ds(HALO + k * WL, WL)] = turned.reshape(WL, seg, -1).astype(BF)
        for cps in back_copies:
            cps.one(pd).start()

    for pd in range(pds):
        fine_attention(pd)

    for k in range(nz - 1):
        share_lon.one(k).wait_recv()
    for k in range(m - 1):
        share_lat.one(k).start()
    loads["wt2"].wait()
    swap(0).wait_recv()
    order = head_order(heads2, hd)
    for k in range(2):
        r["wt2_o"][k] = dot32(r["v_wt2"][k], order).astype(BF)
    for key in ("wo1", "we1", "wr1", "mw"):
        loads[key].wait()

    def fine_tail(pd):
        for cps in back_copies:
            cps.one(pd).wait_recv()
        r["near"][...] = flat(G[pd][:, pl.ds(HALO - s0, rows)])

        def some_rows(k, carry):
            at = pl.ds(pl.multiple_of(k * (cells // 2), 16), cells // 2)
            mixed = dot32(r["B1"][at, :], r["near"][...]).astype(BF)
            attended = (r["F"][pd, at, :].astype(F32) + dot32(mixed, r["v_wo1"][...])).astype(BF)
            normed = layer_norm(attended, r["gm"][...])
            hidden = jax.nn.gelu(dot32(normed, r["v_we1"][...])).astype(BF)
            state = (attended.astype(F32) + dot32(hidden, r["v_wr1"][...])).astype(BF)
            r["state"][pd, at, :] = state.astype(F32)
            return carry

        lax.fori_loop(0, 2, some_rows, 0)
        merged = jnp.concatenate([r["state"][pd, k * few : (k + 1) * few, :] for k in range(4)], axis=1)
        coarse_in = dot32(layer_norm(merged, r["mg"][...]), r["v_mw"][...]).astype(BF)
        r["cin"][pd] = coarse_in
        X[pd, zi] = layer_norm(coarse_in, r["g2"][...])
        gather1_start(pd)

    for pd in range(pds):
        fine_tail(pd)

    for pd in range(pds):
        for z in range(nz):
            Y[pd, core, z, few:] = pad

    def coarse_project(pd):
        def project(z):
            given = X[pd, z]
            S[pd, z, pl.ds(0, few)] = dot32(given, r["wt2_o"][1 - core]).astype(BF)
            cross[0].one(pd, z).start()
            cross[2].one(pd, z).start()
            Y[pd, core, z, pl.ds(0, few)] = dot32(given, r["wt2_o"][core]).astype(BF)
            cross[1].one(pd, z).start()

        def one_chunk(j, carry):
            project(gather1_arrive(pd, j))
            return carry

        project(zi)
        lax.fori_loop(0, nz - 1, one_chunk, 0)

    for pd in range(pds):
        coarse_project(pd)
    for k in range(m - 1):
        share_lat.one(k).wait_recv()
    share_core.one(0).start()
    loads["b2"].wait()

    def coarse_attention(pd, carry):
        for z in range(nz):
            for cps in cross:
                cps.one(pd, z).wait_recv()

        def one_window(w, carry):
            zs = [lax.rem(w + dz, nz) for dz in range(2)]
            pieces = [Y[pd, par, z] for z in zs for par in range(2)]
            pieces += [H[pd, par, z] for z in zs for par in range(2)]
            part = dot32(r["P2"][...], jnp.concatenate(pieces, axis=0))
            total = attend(part, heads2, hd, lambda h: r["v_b2"][h], r["K2"][...])
            r["V"][w] = total.astype(BF)
            return carry

        lax.fori_loop(0, nz, one_window, 0)

        def one_chip(z, carry):
            both = jnp.concatenate([r["V"][z], r["V"][lax.rem(z + nz - 1, nz)]], axis=0)
            back = dot32(r["U2"][...], both).astype(BF)
            for par in range(2):
                C[pd, par, z] = back[par * fewp : (par + 1) * fewp]
                D[pd, par, z] = back[2 * fewp + par * hal : 2 * fewp + (par + 1) * hal]
            return carry

        lax.fori_loop(0, nz, one_chip, 0)
        for k in range(n - 1):
            spread_here.one(pd, k).start()
        for k in range(n):
            spread_next.one(pd, k).start()
        M[pd, lon] = C[pd, core, zi, pl.ds(0, few)]
        return carry

    coarse_attention(0, 0)
    coarse_attention(1, 0)
    share_core.one(0).wait_recv()

    def coarse_output(pd, carry):
        for k in range(n - 1):
            spread_here.one(pd, k).wait_recv()
        for k in range(n):
            spread_next.one(pd, k).wait_recv()
        value = r["cin"][pd].astype(F32)
        tail = jnp.zeros((few - hal, lanes2), F32)
        for g in range(n):
            part = M[pd, g].astype(F32) + jnp.concatenate([N[pd, g].astype(F32), tail], axis=0)
            rows_g = W[g % 2, :, g // 2]
            rows_g = rows_g.reshape(lanes2, -1) if rows_g.shape[1] % 16 == 0 else flat(rows_g)
            value += dot32(part.astype(BF), rows_g)
        middle = value.astype(BF)
        r["mid"][pd] = middle
        Z[pd, zi] = layer_norm(middle, r["gm2"][...])
        gather2_start(pd)
        return carry

    coarse_output(0, 0)
    coarse_output(1, 0)
    for key in ("we2", "wr2", "up"):
        loads[key].wait()
    swap(1).wait_recv()
    swap(2).wait_recv()

    def coarse_feed(pd):
        def feed(z):
            given = Z[pd, z]
            total = None
            for k in range(2):
                hidden = jax.nn.gelu(dot32(given, r["v_we2"][k])).astype(BF)
                term = dot32(hidden, r["v_wr2"][k])
                total = term if total is None else total + term
            return total

        def one_chunk(j, carry):
            z = gather2_arrive(pd, j)
            Q[pd, z] = feed(z).astype(BF)
            partial_to(pd, z).start()
            return carry

        r["own"][pd] = feed(zi)
        lax.fori_loop(0, nz - 1, one_chunk, 0)

    for pd in range(pds):
        coarse_feed(pd)

    def finish(pd, carry):
        value = r["mid"][pd].astype(F32) + r["own"][pd]
        for k in range(1, nz):
            z = lax.rem(zi + k, nz)
            partial_from(pd, z).wait_recv()
            value += T[pd, z].astype(F32)
        state = value.astype(BF)
        r["cstate"][pd] = state
        expanded = dot32(state, r["v_up"][...])
        channels = expanded.shape[1] // 4
        for k in range(4):
            at = slice(k * few, (k + 1) * few)
            cut = slice(k * channels, (k + 1) * channels)
            r["state"][pd, at, :] = r["state"][pd, at, :] + expanded[:, cut]
        r["blended"][pd] = dot32(r["B2"][...], r["state"][pd].astype(BF)).astype(BF)
        return carry

    lax.fori_loop(0, pds, finish, 0)

    for pd in range(pds):
        for cps in halo_copies + back_copies:
            cps.one(pd).wait_send()
        for z in range(nz):
            for cps in cross:
                cps.one(pd, z).wait_send()
        gather1_drain(pd)
        gather2_drain(pd)
        for k in range(1, nz):
            partial_to(pd, lax.rem(zi + k, nz)).wait_send()
        for k in range(n - 1):
            spread_here.one(pd, k).wait_send()
        for k in range(n):
            spread_next.one(pd, k).wait_send()
    for k in range(nz - 1):
        share_lon.one(k).wait_send()
    for k in range(m - 1):
        share_lat.one(k).wait_send()
    share_core.one(0).wait_send()
    for k in range(3):
        swap(k).wait_send()


def body(
    fine_field,
    offsets,
    fine_prenorm,
    fine_triple,
    fine_bias,
    fine_output,
    fine_midnorm,
    fine_expand,
    fine_reduce,
    merge_gain,
    merge_weight,
    coarse_prenorm,
    coarse_triple,
    coarse_bias,
    coarse_output,
    coarse_midnorm,
    coarse_expand,
    coarse_reduce,
    upsample_weight,
):
    levels, rows, cols, channels = fine_field.shape
    m = lax.axis_size("lat")
    n = lax.axis_size("lon")
    nz = n // 2
    pds = levels // WD
    wide = coarse_output.shape[1]
    heads1, heads2 = fine_bias.shape[0], coarse_bias.shape[0]
    hd = channels // heads1
    lanes2 = coarse_output.shape[0]
    assert cols == WW and rows == 2 * WL and n % 2 == 0 and nz >= 2 and pds == 2
    assert lanes2 == heads2 * hd and lanes2 % m == 0
    half, hc = rows // 2, cols // 2
    seg = WD * cols
    cells = rows * seg
    few = cells // 4
    fewp = up_to(few, 16)
    hal = up_to(HALO * WD * hc, 16)

    x = fine_field.reshape(pds, WD, rows, cols, channels).transpose(0, 2, 1, 3, 4)
    x = x.reshape(pds, rows, seg, channels)
    vmem = pl.BlockSpec(memory_space=pltpu.VMEM)
    hbm = pl.BlockSpec(memory_space=pl.ANY)
    args = [
        ("off", offsets, pl.BlockSpec(memory_space=pltpu.SMEM)),
        ("x", x, hbm),
        ("g1", fine_prenorm[None], vmem),
        ("wt", fine_triple, hbm),
        ("b1", fine_bias, hbm),
        ("wo1", fine_output, hbm),
        ("gm", fine_midnorm[None], vmem),
        ("we1", fine_expand, hbm),
        ("wr1", fine_reduce, hbm),
        ("mg", merge_gain[None], vmem),
        ("mw", merge_weight, hbm),
        ("g2", coarse_prenorm[None], vmem),
        ("wt2", coarse_triple, hbm),
        ("b2", coarse_bias, hbm),
        ("wo2", coarse_output.reshape(m, lanes2 // m, wide), hbm),
        ("gm2", coarse_midnorm[None], vmem),
        ("we2", coarse_expand, hbm),
        ("wr2", coarse_reduce, hbm),
        ("up", upsample_weight, hbm),
    ]
    outs = [
        ("blended", jax.ShapeDtypeStruct((pds, cells, channels), BF)),
        ("cstate", jax.ShapeDtypeStruct((pds, few, wide), BF)),
    ]
    sem = pltpu.SemaphoreType.DMA
    wide3 = 3 * lanes2
    scratch = [
        ("lsem", sem((14,))),
        ("v_wt", pltpu.VMEM(fine_triple.shape, BF)),
        ("wt_o", pltpu.VMEM(fine_triple.shape, BF)),
        ("v_b1", pltpu.VMEM(fine_bias.shape, F32)),
        ("v_wo1", pltpu.VMEM(fine_output.shape, BF)),
        ("v_we1", pltpu.VMEM(fine_expand.shape, BF)),
        ("v_wr1", pltpu.VMEM(fine_reduce.shape, BF)),
        ("v_mw", pltpu.VMEM(merge_weight.shape, BF)),
        ("v_wt2", pltpu.VMEM((2,) + coarse_triple.shape, BF)),
        ("wt2_o", pltpu.VMEM((2,) + coarse_triple.shape, BF)),
        ("v_b2", pltpu.VMEM(coarse_bias.shape, F32)),
        ("v_we2", pltpu.VMEM((2,) + coarse_expand.shape, BF)),
        ("v_wr2", pltpu.VMEM((2,) + coarse_reduce.shape, BF)),
        ("v_up", pltpu.VMEM(upsample_weight.shape, BF)),
        ("W", pltpu.VMEM((2, m, nz, lanes2 // m, wide), BF)),
        ("P1", pltpu.VMEM((WT, 2 * WL * seg), BF)),
        ("U1", pltpu.VMEM((WT, WT), BF)),
        ("B0", pltpu.VMEM((cells, cells), BF)),
        ("B1", pltpu.VMEM((cells, 2 * cells), BF)),
        ("B2", pltpu.VMEM((cells, cells), BF)),
        ("P2", pltpu.VMEM((WT, 4 * fewp + 4 * hal), BF)),
        ("U2", pltpu.VMEM((2 * fewp + 2 * hal, 2 * WT), BF)),
        ("K1", pltpu.VMEM((rows // WL, WT, WT), F32)),
        ("K2", pltpu.VMEM((WT, WT), F32)),
        ("F", pltpu.VMEM((pds, cells, channels), BF)),
        ("A", pltpu.VMEM((cells, channels), BF)),
        ("tri", pltpu.VMEM((cells, 3 * channels), BF)),
        ("near", pltpu.VMEM((2 * cells, channels), BF)),
        ("state", pltpu.VMEM((pds, cells, channels), F32)),
        ("cin", pltpu.VMEM((pds, few, wide), BF)),
        ("X", pltpu.VMEM((pds, nz, few, wide), BF)),
        ("Y", pltpu.VMEM((pds, 2, nz, fewp, wide3), BF)),
        ("S", pltpu.VMEM((pds, nz, fewp, wide3), BF)),
        ("H", pltpu.VMEM((pds, 2, nz, hal, wide3), BF)),
        ("V", pltpu.VMEM((nz, WT, lanes2), BF)),
        ("C", pltpu.VMEM((pds, 2, nz, fewp, lanes2), BF)),
        ("D", pltpu.VMEM((pds, 2, nz, hal, lanes2), BF)),
        ("M", pltpu.VMEM((pds, n, few, lanes2), BF)),
        ("N", pltpu.VMEM((pds, n, hal, lanes2), BF)),
        ("mid", pltpu.VMEM((pds, few, wide), BF)),
        ("Z", pltpu.VMEM((pds, nz, few, wide), BF)),
        ("own", pltpu.VMEM((pds, few, wide), F32)),
        ("Q", pltpu.VMEM((pds, nz, few, wide), BF)),
        ("T", pltpu.VMEM((pds, nz, few, wide), BF)),
    ]
    for pd in range(pds):
        for name in ("E", "G"):
            scratch.append((name + str(pd), pltpu.VMEM((2, rows + HALO, seg, channels), BF)))
    for name, shape in (("h", (pds,)), ("b", (pds,)), ("c", (pds, nz))):
        for k in range(3):
            scratch += [("%ss%d" % (name, k), sem(shape)), ("%sr%d" % (name, k), sem(shape))]
    for s, d, shape in (
        ("ws0", "wr0", (nz - 1,)),
        ("ws1", "wr1s", (m - 1,)),
        ("ws2", "wr2s", (1,)),
        ("ss", "sr", (3,)),
        ("as0", "ar0", (pds, 2, nz - 1)),
        ("as1", "ar1", (pds, 2, nz - 1)),
        ("ds0", "dr0", (pds, n - 1)),
        ("ds1", "dr1", (pds, n)),
        ("rs0", "rr0", (pds, nz)),
    ):
        scratch += [(s, sem(shape)), (d, sem(shape))]

    cfg = dict(m=m, n=n, pds=pds, rows=rows, cols=cols, heads1=heads1, heads2=heads2, hd=hd)
    names = [a[0] for a in args] + [o[0] for o in outs] + [s[0] for s in scratch]
    blended, state = pl.pallas_call(
        functools.partial(step_kernel, cfg, names),
        out_shape=[o[1] for o in outs],
        in_specs=[a[2] for a in args],
        out_specs=[vmem, vmem],
        scratch_shapes=[s[1] for s in scratch],
        compiler_params=pltpu.CompilerParams(
            collective_id=0, has_side_effects=True, vmem_limit_bytes=63 << 20
        ),
    )(*[a[1] for a in args])
    blended = blended.reshape(pds, rows, WD, cols, channels).transpose(0, 2, 1, 3, 4)
    state = state.reshape(pds, half, WD, hc, wide).transpose(0, 2, 1, 3, 4)
    return (
        blended.reshape(levels, rows, cols, channels),
        state.reshape(levels, half, hc, wide),
    )


def solution(mesh):
    placed = (
        P(None, "lat", "lon", None),
        P(),
        P(),
        P(),
        P(),
        P(),
        P(),
        P(),
        P(),
        P(),
        P(),
        P(),
        P(None, "lon"),
        P("lon", None, None),
        P("lon", None),
        P(),
        P(None, "lon"),
        P("lon", None),
        P(),
    )
    return jax.shard_map(
        body,
        mesh=mesh,
        in_specs=placed,
        out_specs=(P(None, "lat", "lon", None), P(None, "lat", "lon", None)),
        check_vma=False,
    )
```

```python
import functools

import jax
import jax.numpy as jnp
from jax import lax
from jax.experimental import pallas as pl
from jax.experimental.pallas import tpu as pltpu
from jax.sharding import PartitionSpec as P

WD = 2
WL = 6
WW = 12
WT = 144
HALO = WL - 1

epsilon = 1e-05
masked_score = -1e30
BF = jnp.bfloat16
F32 = jnp.float32
I32 = jnp.int32
MESH = pl.DeviceIdType.MESH


def up_to(value, step):
    return -(-value // step) * step


def layer_norm(values, gain_vec):
    values = values.astype(F32)
    center = jnp.mean(values, axis=-1, keepdims=True)
    offset_vals = values - center
    spread = jnp.mean(offset_vals * offset_vals, axis=-1, keepdims=True)
    return (offset_vals * lax.rsqrt(spread + epsilon) * gain_vec).astype(BF)


def dot32(left, right):
    return jnp.dot(left, right, preferred_element_type=F32)


def down(count):
    return lax.broadcasted_iota(I32, (count, 1), 0)


def along(count):
    return lax.broadcasted_iota(I32, (1, count), 1)


def one_hot(row_key, col_key):
    return (row_key == col_key).astype(F32).astype(BF)


def flat(block):
    return block.astype(F32).reshape(-1, block.shape[-1]).astype(BF)


def window_mask(limit):
    row = (lax.broadcasted_iota(I32, (WT, WT), 0) // WW) % WL
    col = (lax.broadcasted_iota(I32, (WT, WT), 1) // WW) % WL
    row_in = (row >= limit).astype(I32)
    col_in = (col >= limit).astype(I32)
    return jnp.where(row_in == col_in, 0.0, masked_score)


def head_order(heads, head_dim):
    lanes = heads * head_dim
    width = 3 * lanes
    row = down(width)
    col = along(width)
    origin = ((col % lanes) // head_dim) * (3 * head_dim) + (col // lanes) * head_dim + col % head_dim
    return one_hot(row, origin)


def attend(part, heads, head_dim, bias_at, place_mask):
    lanes = heads * head_dim
    queries = part[:, :lanes].astype(F32)
    keys_all = part[:, lanes : 2 * lanes].astype(BF)
    values = part[:, 2 * lanes :].astype(BF)
    lane = lax.broadcasted_iota(I32, (WT, lanes), 1) // head_dim
    total = None
    for h in range(heads):
        mine = jnp.where(lane == h, queries, 0.0).astype(BF)
        scores = lax.dot_general(
            mine, keys_all, (((1,), (1,)), ((), ())), preferred_element_type=F32
        )
        scores = scores * head_dim ** (-0.5) + bias_at(h) + place_mask
        top = jnp.max(scores, axis=-1, keepdims=True)
        lifted = jnp.exp(scores - top)
        weight_sum = jnp.sum(lifted, axis=-1, keepdims=True)
        mixed = dot32(lifted.astype(BF), values) / weight_sum
        mixed = jnp.where(lane == h, mixed, 0.0)
        total = mixed if total is None else total + mixed
    return total


class Copies:
    def __init__(self, send, recv, make):
        self.send, self.recv, self.make = send, recv, make

    def one(self, *index):
        src, dst, device = self.make(*index)
        return pltpu.make_async_remote_copy(
            src, dst, self.send.at[index], self.recv.at[index], device_id=device, device_id_type=MESH
        )


def blocked(index, cells, few, per_row, hc):
    block, cell = index // few, index % few
    i = (cell // per_row) * 2 + block % 2
    j = (cell % hc) * 2 + block // 2
    return i * WD + (cell // hc) % WD, j


def arrange_kernel(fine_ref, coarse_ref, fine_out, coarse_out):
    pds, cells, _ = fine_ref.shape
    few = coarse_ref.shape[1]
    _, cols, levels, _ = fine_out.shape
    hc = cols // 2
    per_row = WD * hc
    q = along(pds * cells)
    ia, j = blocked(q % cells, cells, few, per_row, hc)
    chosen = one_hot(down(pds * cells), ((ia // WD) * cols + j) * levels + (q // cells) * WD + ia % WD)
    fine_out[...] = dot32(chosen, flat(fine_ref[...])).reshape(fine_out.shape).astype(BF)
    q = along(pds * few)
    cell = q % few
    chosen = one_hot(
        down(pds * few),
        ((cell // per_row) * hc + cell % hc) * levels + (q // few) * WD + (cell // hc) % WD,
    )
    coarse_out[...] = dot32(chosen, flat(coarse_ref[...])).reshape(coarse_out.shape).astype(BF)


def step_kernel(cfg, names, *refs):
    r = dict(zip(names, refs))
    m, n, nz = cfg["m"], cfg["n"], cfg["n"] // 2
    pds, rows, cols = cfg["pds"], cfg["rows"], cfg["cols"]
    seg = WD * cols
    cells = rows * seg
    half = rows // 2
    hc = cols // 2
    per_row = WD * hc
    few = half * per_row
    fewp = up_to(few, 16)
    hal = up_to(HALO * per_row, 16)
    heads1, heads2, hd = cfg["heads1"], cfg["heads2"], cfg["hd"]
    lanes2 = heads2 * hd
    wins = rows // WL
    lat = lax.axis_index("lat")
    lon = lax.axis_index("lon")
    zi, core = lon // 2, lon % 2
    buddy = lon + 1 - 2 * core
    s0, s1, s2, s3 = r["off"][0], r["off"][1], r["off"][2], r["off"][3]

    def dev(dlat, dlon):
        return (lax.rem(lat + dlat + m, m), lax.rem(lon + dlon + n, n))

    greet = {(0, d) for d in range(1, n)}
    greet |= {(d % m, e) for d in (-1, 1) for e in range(n)}
    greet |= {(d, 0) for d in range(1, m)}
    greet -= {(0, 0)}
    barrier = pltpu.get_barrier_semaphore()
    for dlat, dlon in sorted(greet):
        pl.semaphore_signal(barrier, 1, device_id=dev(dlat, dlon), device_id_type=MESH)

    def local(k, src, dst):
        return pltpu.make_async_copy(src, dst, r["lsem"].at[k])

    E = [r["E%d" % pd] for pd in range(pds)]
    G = [r["G%d" % pd] for pd in range(pds)]
    loads = {
        "x": local(0, r["x"], r["v_x"]),
        "wt": local(2, r["wt"], r["v_wt"]),
        "b1": local(3, r["b1"], r["v_b1"]),
        "wo1": local(4, r["wo1"], r["v_wo1"]),
        "we1": local(5, r["we1"], r["v_we1"]),
        "wr1": local(6, r["wr1"], r["v_wr1"]),
        "mw": local(7, r["mw"], r["v_mw"]),
        "wt2": local(8, r["wt2"], r["v_wt2"].at[core]),
        "b2": local(9, r["b2"], r["v_b2"]),
        "we2": local(10, r["we2"], r["v_we2"].at[core]),
        "wr2": local(11, r["wr2"], r["v_wr2"].at[core]),
        "up": local(12, r["up"], r["v_up"]),
        "wo2": local(13, r["wo2"].at[lat], r["W"].at[core, lat, zi]),
    }
    for key in ("x", "wt", "b1", "wo2"):
        loads[key].start()

    halo_copies = [
        Copies(r["hs%d" % k], r["hr%d" % k], make)
        for k, make in enumerate(
            (
                lambda pd: (E[pd].at[0, pl.ds(0, rows)], E[pd].at[1, pl.ds(0, rows)], dev(0, -1)),
                lambda pd: (E[pd].at[0, pl.ds(0, HALO)], E[pd].at[0, pl.ds(rows, HALO)], dev(-1, 0)),
                lambda pd: (E[pd].at[0, pl.ds(0, HALO)], E[pd].at[1, pl.ds(rows, HALO)], dev(-1, -1)),
            )
        )
    ]
    low = rows - HALO
    back_copies = [
        Copies(r["bs%d" % k], r["br%d" % k], make)
        for k, make in enumerate(
            (
                lambda pd: (G[pd].at[0, pl.ds(HALO, rows)], G[pd].at[1, pl.ds(HALO, rows)], dev(0, 1)),
                lambda pd: (G[pd].at[0, pl.ds(HALO + low, HALO)], G[pd].at[0, pl.ds(0, HALO)], dev(1, 0)),
                lambda pd: (G[pd].at[0, pl.ds(HALO + low, HALO)], G[pd].at[1, pl.ds(0, HALO)], dev(1, 1)),
            )
        )
    ]
    W = r["W"]
    share_lon = Copies(
        r["ws0"], r["wr0"], lambda k: (W.at[core, lat, zi], W.at[core, lat, zi], dev(0, 2 * (k + 1)))
    )
    share_lat = Copies(r["ws1"], r["wr1s"], lambda k: (W.at[core, lat], W.at[core, lat], dev(k + 1, 0)))
    share_core = Copies(r["ws2"], r["wr2s"], lambda k: (W.at[core], W.at[core], (lat, buddy)))

    def swap(k):
        name = ("wt2", "we2", "wr2")[k]
        return pltpu.make_async_remote_copy(
            r[name],
            r["v_" + name].at[core],
            r["ss"].at[k],
            r["sr"].at[k],
            device_id=(lat, buddy),
            device_id_type=MESH,
        )

    X, Y, S, H = r["X"], r["Y"], r["S"], r["H"]

    def relay(buf, sends, recvs):
        def hop(pd, z, way, reach):
            step = 2 - 4 * way
            return pltpu.make_async_remote_copy(
                buf.at[pd, z],
                buf.at[pd, z],
                r[sends].at[pd, way, reach - 1],
                r[recvs].at[pd, way, reach - 1],
                device_id=(lat, lon + step),
                device_id_type=MESH,
            )

        def pass_on(pd, z, way, reach, act):
            @pl.when(jnp.where(way == 0, zi < nz - 1, zi > 0))
            def _():
                act(hop(pd, z, way, reach))

        def start(pd):
            for way in range(2):
                pass_on(pd, zi, way, 1, lambda c: c.start())

        def turn(j):
            both = jnp.minimum(zi, nz - 1 - zi)
            even = j < 2 * both
            way = jnp.where(even, j % 2, jnp.where(zi > nz - 1 - zi, 0, 1))
            reach = jnp.where(even, j // 2 + 1, j - both + 1)
            return zi - reach * (1 - 2 * way), way, reach

        def arrive(pd, j):
            z, way, reach = turn(j)
            hop(pd, z, way, reach).wait_recv()

            @pl.when(reach < nz - 1)
            def _():
                pass_on(pd, z, way, reach + 1, lambda c: c.start())

            return z

        def drain(pd):
            def one(j, carry):
                z, way, reach = turn(j)

                @pl.when(reach < nz - 1)
                def _():
                    pass_on(pd, z, way, reach + 1, lambda c: c.wait_send())

                return carry

            for way in range(2):
                pass_on(pd, zi, way, 1, lambda c: c.wait_send())
            lax.fori_loop(0, nz - 1, one, 0)

        return start, arrive, drain

    gather1_start, gather1_arrive, gather1_drain = relay(X, "as0", "ar0")
    cross = [
        Copies(r["cs%d" % k], r["cr%d" % k], make)
        for k, make in enumerate(
            (
                lambda pd, z: (S.at[pd, z], Y.at[pd, core, z], (lat, buddy)),
                lambda pd, z: (Y.at[pd, core, z, pl.ds(0, hal)], H.at[pd, core, z], dev(-1, 0)),
                lambda pd, z: (S.at[pd, z, pl.ds(0, hal)], H.at[pd, core, z], (lax.rem(lat + m - 1, m), buddy)),
            )
        )
    ]
    C, D, M, N = r["C"], r["D"], r["M"], r["N"]

    def to_owner(pd, k):
        owner = lax.rem(lon + k + 1, n)
        return C.at[pd, owner % 2, owner // 2, pl.ds(0, few)], M.at[pd, lon], (lat, owner)

    def to_next(pd, k):
        owner = lax.rem(lon + k, n)
        return D.at[pd, owner % 2, owner // 2], N.at[pd, lon], (lax.rem(lat + 1, m), owner)

    spread_here = Copies(r["ds0"], r["dr0"], to_owner)
    spread_next = Copies(r["ds1"], r["dr1"], to_next)
    Z, Q, T, R = r["Z"], r["Q"], r["T"], r["R"]
    gather2_start, gather2_arrive, gather2_drain = relay(Z, "as1", "ar1")

    def partial(pd, z):
        way = jnp.where(z > zi, 0, 1)
        step = 2 - 4 * way

        def message(dst, recv, target):
            return pltpu.make_async_remote_copy(
                Q.at[pd, z], dst, r["rs0"].at[pd, z], recv, device_id=(lat, target), device_id_type=MESH
            )

        final = message(T.at[pd, way], r["rr0"].at[pd, way], lon + step)
        between = message(R.at[pd, z], r["rr1"].at[pd, z], lon + step)
        direct = message(T.at[pd, 2], r["rr0"].at[pd, 2], 2 * z + core)
        return jnp.abs(z - zi), final, between, direct

    def partial_start(pd, z):
        reach, final, between, direct = partial(pd, z)

        @pl.when(reach == 1)
        def _():
            final.start()

        straight = nz > 2 and pd == pds - 1

        @pl.when((reach > 1) & (reach < (nz - 1 if straight else nz)))
        def _():
            between.start()

        if straight:

            @pl.when(reach == nz - 1)
            def _():
                direct.start()

    def adds(pd, z):
        first = ((z == 0) & (zi == nz - 2)) | ((z == nz - 1) & (zi == 1))
        inner = (zi > 0) & (zi < nz - 1)
        return inner & jnp.logical_not(first) if pd == pds - 1 else inner

    def partial_pass(pd, j):
        above, below = nz - 1 - zi, zi
        up = jnp.where(2 * zi < nz, j < above, j >= below)
        z = jnp.where(
            2 * zi < nz,
            jnp.where(up, zi + 1 + j, zi - 1 - (j - above)),
            jnp.where(up, zi + 1 + (j - below), zi - 1 - j),
        )

        @pl.when(adds(pd, z))
        def _():
            partial(pd, z)[2].wait_recv()
            Q[pd, z] = (r["part"][pd, z] + R[pd, z].astype(F32)).astype(BF)
            partial_start(pd, z)

    piece = WL * seg
    q = down(pds * piece)
    inside = q % piece
    to_pairs = one_hot(
        ((inside // seg) * cols + inside % cols) * (pds * WD) + (q // piece) * WD + (inside % seg) // cols,
        along(pds * piece),
    )
    loads["x"].wait()
    for k in range(wins):
        turned = dot32(to_pairs, flat(r["v_x"][k * WL : (k + 1) * WL]))
        for pd in range(pds):
            E[pd][0, k * WL : (k + 1) * WL] = (
                turned[pd * piece : (pd + 1) * piece].reshape(WL, seg, -1).astype(BF)
            )
    pl.semaphore_wait(barrier, len(greet))
    for pd in range(pds):
        for cps in halo_copies:
            cps.one(pd).start()
    loads["wo2"].wait()
    for k in range(nz - 1):
        share_lon.one(k).start()
    for k in range(3):
        swap(k).start()
    for key in ("we2", "wr2", "wt2", "wo1", "we1", "wr1", "mw", "b2", "up"):
        loads[key].start()

    def place(index):
        return index // (WL * WW), (index // WW) % WL, index % WW

    a, b, c = place(down(WT))
    q = along(2 * WL * seg)
    r["P1"][...] = one_hot(
        (b * WD + a) * 64 + c + s1,
        ((q % (WL * seg)) // cols) * 64 + (q // (WL * seg)) * cols + q % cols,
    )
    a, b, c = place(along(WT))
    row = down(WT)
    r["U1"][...] = one_hot(row, (b * WD + a) * WW + c)

    ia, j = blocked(down(cells), cells, few, per_row, hc)
    q = along(2 * cells)
    r["B1"][...] = one_hot(
        ia * 64 + j - s1 + cols,
        ((q % cells) // cols) * 64 + jnp.where(q < cells, cols, 0) + q % cols,
    )
    q = along(cells)
    r["B0"][...] = one_hot(ia * cols + j, q)
    def own_key(index, size, first):
        return jnp.where(
            index < size, (index // hc + first * WD) * 64 + index % hc, -1
        )

    a, b, c = place(down(WT))
    q = along(4 * fewp + 4 * hal)
    far = q >= 4 * fewp
    qh = q - 4 * fewp
    chunk = jnp.where(far, qh // hal, q // fewp)
    key = jnp.where(far, own_key(qh % hal, HALO * per_row, half), own_key(q % fewp, few, 0))
    r["P2"][...] = one_hot(
        ((b + s2) * WD + a) * 64 + c + s3, jnp.where(key < 0, -1, key + chunk * hc)
    )
    a, b, c = place(along(2 * WT) % WT)
    x = c + s3 - jnp.where(along(2 * WT) < WT, 0, cols)
    col_key = jnp.where((x >= 0) & (x < cols), ((b + s2) * WD + a) * 64 + x, -2)
    q = down(2 * fewp + 2 * hal)
    far = q >= 2 * fewp
    qh = q - 2 * fewp
    chunk = jnp.where(far, qh // hal, q // fewp)
    key = jnp.where(far, own_key(qh % hal, HALO * per_row, half), own_key(q % fewp, few, 0))
    r["U2"][...] = one_hot(jnp.where(key < 0, -1, key + chunk * hc), col_key)

    pad = jnp.zeros((fewp - few, 3 * lanes2), BF)
    for pd in range(pds):
        for z in range(nz):
            S[pd, z, few:] = pad
    for k in range(wins):
        r["K1"][k] = window_mask(rows * m - s0 - lat * rows - k * WL)
    r["K2"][...] = window_mask(half * m - s2 - lat * half)

    group = 4 if heads1 % 4 == 0 else heads1
    width = 3 * group * hd
    loads["wt"].wait()
    order = head_order(group, hd)
    for g in range(heads1 // group):
        cut = slice(g * width, (g + 1) * width)
        r["wt_o"][:, cut] = dot32(r["v_wt"][:, cut], order).astype(BF)
    for pd in range(pds):
        r["F"][pd] = dot32(r["B0"][...], flat(E[pd][0, :rows])).astype(BF)
    loads["b1"].wait()

    def fine_attention(pd):
        for cps in halo_copies:
            cps.one(pd).wait_recv()
        for k in range(wins):
            near = flat(E[pd][:, pl.ds(s0 + k * WL, WL)])
            framed = dot32(r["P1"][...], near)
            r["A"][pl.ds(k * WT, WT), :] = layer_norm(framed, r["g1"][...])
        r["tri"][...] = dot32(r["A"][...], r["wt_o"][...]).astype(BF)

        def one_group(g, carry):
            for k in range(wins):
                part = r["tri"][pl.ds(k * WT, WT), pl.ds(pl.multiple_of(g * width, 128), width)]
                total = attend(part, group, hd, lambda h: r["v_b1"][g * group + h], r["K1"][k])
                r["A"][pl.ds(k * WT, WT), pl.ds(pl.multiple_of(g * group * hd, 128), group * hd)] = (
                    total.astype(BF)
                )
            return carry

        lax.fori_loop(0, heads1 // group, one_group, 0)
        for k in range(wins):
            turned = dot32(r["U1"][...], r["A"][pl.ds(k * WT, WT), :])
            G[pd][0, pl.ds(HALO + k * WL, WL)] = turned.reshape(WL, seg, -1).astype(BF)
        for cps in back_copies:
            cps.one(pd).start()

    for pd in range(pds):
        fine_attention(pd)

    for k in range(nz - 1):
        share_lon.one(k).wait_recv()
    for k in range(m - 1):
        share_lat.one(k).start()
    loads["wt2"].wait()
    swap(0).wait_recv()
    order = head_order(heads2, hd)
    for k in range(2):
        r["wt2_o"][k] = dot32(r["v_wt2"][k], order).astype(BF)
    for key in ("wo1", "we1", "wr1", "mw"):
        loads[key].wait()

    def fine_tail(pd):
        for cps in back_copies:
            cps.one(pd).wait_recv()
        r["near"][...] = flat(G[pd][:, pl.ds(HALO - s0, rows)])

        def some_rows(k, carry):
            at = pl.ds(pl.multiple_of(k * (cells // 2), 16), cells // 2)
            mixed = dot32(r["B1"][at, :], r["near"][...]).astype(BF)
            attended = (r["F"][pd, at, :].astype(F32) + dot32(mixed, r["v_wo1"][...])).astype(BF)
            normed = layer_norm(attended, r["gm"][...])
            hidden = jax.nn.gelu(dot32(normed, r["v_we1"][...])).astype(BF)
            state = (attended.astype(F32) + dot32(hidden, r["v_wr1"][...])).astype(BF)
            r["state"][pd, at, :] = state.astype(F32)
            return carry

        lax.fori_loop(0, 2, some_rows, 0)
        merged = jnp.concatenate([r["state"][pd, k * few : (k + 1) * few, :] for k in range(4)], axis=1)
        coarse_in = dot32(layer_norm(merged, r["mg"][...]), r["v_mw"][...]).astype(BF)
        r["cin"][pd] = coarse_in
        X[pd, zi] = layer_norm(coarse_in, r["g2"][...])
        gather1_start(pd)

    for pd in range(pds):
        fine_tail(pd)

    for pd in range(pds):
        for z in range(nz):
            Y[pd, core, z, few:] = pad

    def coarse_project(pd):
        def project(z):
            given = X[pd, z]
            S[pd, z, pl.ds(0, few)] = dot32(given, r["wt2_o"][1 - core]).astype(BF)
            cross[0].one(pd, z).start()
            cross[2].one(pd, z).start()
            Y[pd, core, z, pl.ds(0, few)] = dot32(given, r["wt2_o"][core]).astype(BF)
            cross[1].one(pd, z).start()

        def one_chunk(j, carry):
            project(gather1_arrive(pd, j))
            return carry

        project(zi)
        lax.fori_loop(0, nz - 1, one_chunk, 0)

    for pd in range(pds):
        coarse_project(pd)
    for k in range(m - 1):
        share_lat.one(k).wait_recv()
    share_core.one(0).start()
    loads["b2"].wait()

    def coarse_attention(pd, carry):
        for z in range(nz):
            for cps in cross:
                cps.one(pd, z).wait_recv()

        def one_window(w, carry):
            zs = [lax.rem(w + dz, nz) for dz in range(2)]
            pieces = [Y[pd, par, z] for z in zs for par in range(2)]
            pieces += [H[pd, par, z] for z in zs for par in range(2)]
            part = dot32(r["P2"][...], jnp.concatenate(pieces, axis=0))
            total = attend(part, heads2, hd, lambda h: r["v_b2"][h], r["K2"][...])
            r["V"][w] = total.astype(BF)
            return carry

        lax.fori_loop(0, nz, one_window, 0)

        def one_chip(z, carry):
            both = jnp.concatenate([r["V"][z], r["V"][lax.rem(z + nz - 1, nz)]], axis=0)
            back = dot32(r["U2"][...], both).astype(BF)
            for par in range(2):
                C[pd, par, z] = back[par * fewp : (par + 1) * fewp]
                D[pd, par, z] = back[2 * fewp + par * hal : 2 * fewp + (par + 1) * hal]
            return carry

        lax.fori_loop(0, nz, one_chip, 0)
        for k in range(n - 1):
            spread_here.one(pd, k).start()
        for k in range(n):
            spread_next.one(pd, k).start()
        M[pd, lon] = C[pd, core, zi, pl.ds(0, few)]
        return carry

    coarse_attention(0, 0)
    coarse_attention(1, 0)
    share_core.one(0).wait_recv()

    def coarse_output(pd, carry):
        for k in range(n - 1):
            spread_here.one(pd, k).wait_recv()
        for k in range(n):
            spread_next.one(pd, k).wait_recv()
        value = r["cin"][pd].astype(F32)
        tail = jnp.zeros((few - hal, lanes2), F32)
        for g in range(n):
            part = M[pd, g].astype(F32) + jnp.concatenate([N[pd, g].astype(F32), tail], axis=0)
            rows_g = W[g % 2, :, g // 2]
            rows_g = rows_g.reshape(lanes2, -1) if rows_g.shape[1] % 16 == 0 else flat(rows_g)
            value += dot32(part.astype(BF), rows_g)
        middle = value.astype(BF)
        r["mid"][pd] = middle
        Z[pd, zi] = layer_norm(middle, r["gm2"][...])
        gather2_start(pd)
        return carry

    coarse_output(0, 0)
    coarse_output(1, 0)
    for key in ("we2", "wr2", "up"):
        loads[key].wait()
    swap(1).wait_recv()
    swap(2).wait_recv()

    def coarse_feed(pd):
        def feed(z):
            given = Z[pd, z]
            total = None
            for k in range(2):
                hidden = jax.nn.gelu(dot32(given, r["v_we2"][k])).astype(BF)
                term = dot32(hidden, r["v_wr2"][k])
                total = term if total is None else total + term
            return total

        def one_chunk(j, carry):
            z = gather2_arrive(pd, j)
            term = feed(z)

            @pl.when(adds(pd, z))
            def _():
                r["part"][pd, z] = term

            @pl.when(jnp.logical_not(adds(pd, z)))
            def _():
                Q[pd, z] = term.astype(BF)
                partial_start(pd, z)

            if pd > 0:
                partial_pass(pd - 1, j)
            return carry

        r["own"][pd] = feed(zi)
        lax.fori_loop(0, nz - 1, one_chunk, 0)

    for pd in range(pds):
        coarse_feed(pd)

    def pass_last(j, carry):
        partial_pass(pds - 1, j)
        return carry

    lax.fori_loop(0, nz - 1, pass_last, 0)

    def finish(pd):
        r["sum"][...] = r["mid"][pd].astype(F32) + r["own"][pd]
        for way in range(3 if nz > 2 and pd == pds - 1 else 2):
            end = (zi == 0) | (zi == nz - 1)

            @pl.when((zi > 0, zi < nz - 1, end)[way])
            def _():
                pltpu.make_async_remote_copy(
                    Q.at[pd, zi],
                    T.at[pd, way],
                    r["rs0"].at[pd, zi],
                    r["rr0"].at[pd, way],
                    device_id=(lat, buddy),
                    device_id_type=MESH,
                ).wait_recv()
                r["sum"][...] = r["sum"][...] + T[pd, way].astype(F32)

        value = r["sum"][...]
        state = value.astype(BF)
        r["cstate"][pd] = state
        expanded = dot32(state, r["v_up"][...])
        channels = expanded.shape[1] // 4
        for k in range(4):
            at = slice(k * few, (k + 1) * few)
            cut = slice(k * channels, (k + 1) * channels)
            r["blended"][pd, at, :] = (r["state"][pd, at, :] + expanded[:, cut]).astype(BF)

    for pd in range(pds):
        finish(pd)

    for pd in range(pds):
        for cps in halo_copies + back_copies:
            cps.one(pd).wait_send()
        for z in range(nz):
            for cps in cross:
                cps.one(pd, z).wait_send()
        gather1_drain(pd)
        gather2_drain(pd)
        for k in range(1, nz):
            partial(pd, lax.rem(zi + k, nz))[1].wait_send()
        for k in range(n - 1):
            spread_here.one(pd, k).wait_send()
        for k in range(n):
            spread_next.one(pd, k).wait_send()
    for k in range(nz - 1):
        share_lon.one(k).wait_send()
    for k in range(m - 1):
        share_lat.one(k).wait_send()
    share_core.one(0).wait_send()
    for k in range(3):
        swap(k).wait_send()


def body(
    fine_field,
    offsets,
    fine_prenorm,
    fine_triple,
    fine_bias,
    fine_output,
    fine_midnorm,
    fine_expand,
    fine_reduce,
    merge_gain,
    merge_weight,
    coarse_prenorm,
    coarse_triple,
    coarse_bias,
    coarse_output,
    coarse_midnorm,
    coarse_expand,
    coarse_reduce,
    upsample_weight,
):
    levels, rows, cols, channels = fine_field.shape
    m = lax.axis_size("lat")
    n = lax.axis_size("lon")
    nz = n // 2
    pds = levels // WD
    wide = coarse_output.shape[1]
    heads1, heads2 = fine_bias.shape[0], coarse_bias.shape[0]
    hd = channels // heads1
    lanes2 = coarse_output.shape[0]
    assert cols == WW and rows == 2 * WL and n % 2 == 0 and nz >= 2 and pds == 2
    assert lanes2 == heads2 * hd and lanes2 % m == 0
    half, hc = rows // 2, cols // 2
    seg = WD * cols
    cells = rows * seg
    few = cells // 4
    fewp = up_to(few, 16)
    hal = up_to(HALO * WD * hc, 16)

    x = fine_field.transpose(1, 2, 0, 3)
    vmem = pl.BlockSpec(memory_space=pltpu.VMEM)
    hbm = pl.BlockSpec(memory_space=pl.ANY)
    args = [
        ("off", offsets, pl.BlockSpec(memory_space=pltpu.SMEM)),
        ("x", x, hbm),
        ("g1", fine_prenorm[None], vmem),
        ("wt", fine_triple, hbm),
        ("b1", fine_bias, hbm),
        ("wo1", fine_output, hbm),
        ("gm", fine_midnorm[None], vmem),
        ("we1", fine_expand, hbm),
        ("wr1", fine_reduce, hbm),
        ("mg", merge_gain[None], vmem),
        ("mw", merge_weight, hbm),
        ("g2", coarse_prenorm[None], vmem),
        ("wt2", coarse_triple, hbm),
        ("b2", coarse_bias, hbm),
        ("wo2", coarse_output.reshape(m, lanes2 // m, wide), hbm),
        ("gm2", coarse_midnorm[None], vmem),
        ("we2", coarse_expand, hbm),
        ("wr2", coarse_reduce, hbm),
        ("up", upsample_weight, hbm),
    ]
    outs = [
        ("blended", jax.ShapeDtypeStruct((pds, cells, channels), BF)),
        ("cstate", jax.ShapeDtypeStruct((pds, few, wide), BF)),
    ]
    sem = pltpu.SemaphoreType.DMA
    wide3 = 3 * lanes2
    scratch = [
        ("lsem", sem((14,))),
        ("v_wt", pltpu.VMEM(fine_triple.shape, BF)),
        ("wt_o", pltpu.VMEM(fine_triple.shape, BF)),
        ("v_b1", pltpu.VMEM(fine_bias.shape, F32)),
        ("v_wo1", pltpu.VMEM(fine_output.shape, BF)),
        ("v_we1", pltpu.VMEM(fine_expand.shape, BF)),
        ("v_wr1", pltpu.VMEM(fine_reduce.shape, BF)),
        ("v_mw", pltpu.VMEM(merge_weight.shape, BF)),
        ("v_wt2", pltpu.VMEM((2,) + coarse_triple.shape, BF)),
        ("wt2_o", pltpu.VMEM((2,) + coarse_triple.shape, BF)),
        ("v_b2", pltpu.VMEM(coarse_bias.shape, F32)),
        ("v_we2", pltpu.VMEM((2,) + coarse_expand.shape, BF)),
        ("v_wr2", pltpu.VMEM((2,) + coarse_reduce.shape, BF)),
        ("v_up", pltpu.VMEM(upsample_weight.shape, BF)),
        ("W", pltpu.VMEM((2, m, nz, lanes2 // m, wide), BF)),
        ("P1", pltpu.VMEM((WT, 2 * WL * seg), BF)),
        ("U1", pltpu.VMEM((WT, WT), BF)),
        ("B0", pltpu.VMEM((cells, cells), BF)),
        ("B1", pltpu.VMEM((cells, 2 * cells), BF)),
        ("v_x", pltpu.VMEM(x.shape, BF)),
        ("P2", pltpu.VMEM((WT, 4 * fewp + 4 * hal), BF)),
        ("U2", pltpu.VMEM((2 * fewp + 2 * hal, 2 * WT), BF)),
        ("K1", pltpu.VMEM((rows // WL, WT, WT), F32)),
        ("K2", pltpu.VMEM((WT, WT), F32)),
        ("F", pltpu.VMEM((pds, cells, channels), BF)),
        ("A", pltpu.VMEM((cells, channels), BF)),
        ("tri", pltpu.VMEM((cells, 3 * channels), BF)),
        ("near", pltpu.VMEM((2 * cells, channels), BF)),
        ("state", pltpu.VMEM((pds, cells, channels), F32)),
        ("cin", pltpu.VMEM((pds, few, wide), BF)),
        ("X", pltpu.VMEM((pds, nz, few, wide), BF)),
        ("Y", pltpu.VMEM((pds, 2, nz, fewp, wide3), BF)),
        ("S", pltpu.VMEM((pds, nz, fewp, wide3), BF)),
        ("H", pltpu.VMEM((pds, 2, nz, hal, wide3), BF)),
        ("V", pltpu.VMEM((nz, WT, lanes2), BF)),
        ("C", pltpu.VMEM((pds, 2, nz, fewp, lanes2), BF)),
        ("D", pltpu.VMEM((pds, 2, nz, hal, lanes2), BF)),
        ("M", pltpu.VMEM((pds, n, few, lanes2), BF)),
        ("N", pltpu.VMEM((pds, n, hal, lanes2), BF)),
        ("mid", pltpu.VMEM((pds, few, wide), BF)),
        ("Z", pltpu.VMEM((pds, nz, few, wide), BF)),
        ("own", pltpu.VMEM((pds, few, wide), F32)),
        ("Q", pltpu.VMEM((pds, nz, few, wide), BF)),
        ("T", pltpu.VMEM((pds, 3, few, wide), BF)),
        ("R", pltpu.VMEM((pds, nz, few, wide), BF)),
        ("part", pltpu.VMEM((pds, nz, few, wide), F32)),
        ("sum", pltpu.VMEM((few, wide), F32)),
    ]
    for pd in range(pds):
        for name in ("E", "G"):
            scratch.append((name + str(pd), pltpu.VMEM((2, rows + HALO, seg, channels), BF)))
    for name, shape in (("h", (pds,)), ("b", (pds,)), ("c", (pds, nz))):
        for k in range(3):
            scratch += [("%ss%d" % (name, k), sem(shape)), ("%sr%d" % (name, k), sem(shape))]
    for s, d, shape in (
        ("ws0", "wr0", (nz - 1,)),
        ("ws1", "wr1s", (m - 1,)),
        ("ws2", "wr2s", (1,)),
        ("ss", "sr", (3,)),
        ("as0", "ar0", (pds, 2, nz - 1)),
        ("as1", "ar1", (pds, 2, nz - 1)),
        ("ds0", "dr0", (pds, n - 1)),
        ("ds1", "dr1", (pds, n)),
    ):
        scratch += [(s, sem(shape)), (d, sem(shape))]
    scratch += [("rs0", sem((pds, nz))), ("rr0", sem((pds, 3))), ("rr1", sem((pds, nz)))]

    cfg = dict(m=m, n=n, pds=pds, rows=rows, cols=cols, heads1=heads1, heads2=heads2, hd=hd)
    names = [a[0] for a in args] + [o[0] for o in outs] + [s[0] for s in scratch]
    blended, state = pl.pallas_call(
        functools.partial(step_kernel, cfg, names),
        out_shape=[o[1] for o in outs],
        in_specs=[a[2] for a in args],
        out_specs=[vmem, vmem],
        scratch_shapes=[s[1] for s in scratch],
        compiler_params=pltpu.CompilerParams(
            collective_id=0, has_side_effects=True, vmem_limit_bytes=63 << 20
        ),
    )(*[a[1] for a in args])
    blended, state = pl.pallas_call(
        arrange_kernel,
        out_shape=[
            jax.ShapeDtypeStruct(x.shape, BF),
            jax.ShapeDtypeStruct((half, hc, levels, wide), BF),
        ],
        in_specs=[vmem, vmem],
        out_specs=[vmem, vmem],
    )(blended, state)
    return blended.transpose(2, 0, 1, 3), state.transpose(2, 0, 1, 3)


def solution(mesh):
    placed = (
        P(None, "lat", "lon", None),
        P(),
        P(),
        P(),
        P(),
        P(),
        P(),
        P(),
        P(),
        P(),
        P(),
        P(),
        P(None, "lon"),
        P("lon", None, None),
        P("lon", None),
        P(),
        P(None, "lon"),
        P("lon", None),
        P(),
    )
    return jax.shard_map(
        body,
        mesh=mesh,
        in_specs=placed,
        out_specs=(P(None, "lat", "lon", None), P(None, "lat", "lon", None)),
        check_vma=False,
    )
```

```python
import functools

import jax
import jax.numpy as jnp
from jax import lax
from jax.experimental import pallas as pl
from jax.experimental.pallas import tpu as pltpu
from jax.sharding import PartitionSpec as P

WD = 2
WL = 6
WW = 12
WT = 144
HALO = WL - 1

epsilon = 1e-05
masked_score = -1e30
BF = jnp.bfloat16
F32 = jnp.float32
I32 = jnp.int32
MESH = pl.DeviceIdType.MESH


def up_to(value, step):
    return -(-value // step) * step


def layer_norm(values, gain_vec):
    values = values.astype(F32)
    center = jnp.mean(values, axis=-1, keepdims=True)
    offset_vals = values - center
    spread = jnp.mean(offset_vals * offset_vals, axis=-1, keepdims=True)
    return (offset_vals * lax.rsqrt(spread + epsilon) * gain_vec).astype(BF)


def dot32(left, right):
    return jnp.dot(left, right, preferred_element_type=F32)


def down(count):
    return lax.broadcasted_iota(I32, (count, 1), 0)


def along(count):
    return lax.broadcasted_iota(I32, (1, count), 1)


def one_hot(row_key, col_key):
    return (row_key == col_key).astype(F32).astype(BF)


def flat(block):
    return block.astype(F32).reshape(-1, block.shape[-1]).astype(BF)


def window_mask(limit):
    row = (lax.broadcasted_iota(I32, (WT, WT), 0) // WW) % WL
    col = (lax.broadcasted_iota(I32, (WT, WT), 1) // WW) % WL
    row_in = (row >= limit).astype(I32)
    col_in = (col >= limit).astype(I32)
    return jnp.where(row_in == col_in, 0.0, masked_score)


def head_order(heads, head_dim):
    lanes = heads * head_dim
    width = 3 * lanes
    row = down(width)
    col = along(width)
    origin = ((col % lanes) // head_dim) * (3 * head_dim) + (col // lanes) * head_dim + col % head_dim
    return one_hot(row, origin)


def attend(part, heads, head_dim, bias_at, place_mask):
    lanes = heads * head_dim
    queries = part[:, :lanes].astype(F32)
    keys_all = part[:, lanes : 2 * lanes].astype(BF)
    values = part[:, 2 * lanes :].astype(BF)
    lane = lax.broadcasted_iota(I32, (WT, lanes), 1) // head_dim
    total = None
    for h in range(heads):
        mine = jnp.where(lane == h, queries, 0.0).astype(BF)
        scores = lax.dot_general(
            mine, keys_all, (((1,), (1,)), ((), ())), preferred_element_type=F32
        )
        scores = scores * head_dim ** (-0.5) + bias_at(h) + place_mask
        top = jnp.max(scores, axis=-1, keepdims=True)
        lifted = jnp.exp(scores - top)
        weight_sum = jnp.sum(lifted, axis=-1, keepdims=True)
        mixed = dot32(lifted.astype(BF), values) / weight_sum
        mixed = jnp.where(lane == h, mixed, 0.0)
        total = mixed if total is None else total + mixed
    return total


class Copies:
    def __init__(self, send, recv, make):
        self.send, self.recv, self.make = send, recv, make

    def one(self, *index):
        src, dst, device = self.make(*index)
        return pltpu.make_async_remote_copy(
            src, dst, self.send.at[index], self.recv.at[index], device_id=device, device_id_type=MESH
        )


def blocked(index, cells, few, per_row, hc):
    block, cell = index // few, index % few
    i = (cell // per_row) * 2 + block % 2
    j = (cell % hc) * 2 + block // 2
    return i * WD + (cell // hc) % WD, j


def arrange_kernel(fine_ref, coarse_ref, fine_out, coarse_out):
    pds, cells, _ = fine_ref.shape
    few = coarse_ref.shape[1]
    _, cols, levels, _ = fine_out.shape
    hc = cols // 2
    per_row = WD * hc
    q = along(pds * cells)
    ia, j = blocked(q % cells, cells, few, per_row, hc)
    chosen = one_hot(down(pds * cells), ((ia // WD) * cols + j) * levels + (q // cells) * WD + ia % WD)
    fine_out[...] = dot32(chosen, flat(fine_ref[...])).reshape(fine_out.shape).astype(BF)
    q = along(pds * few)
    cell = q % few
    chosen = one_hot(
        down(pds * few),
        ((cell // per_row) * hc + cell % hc) * levels + (q // few) * WD + (cell // hc) % WD,
    )
    coarse_out[...] = dot32(chosen, flat(coarse_ref[...])).reshape(coarse_out.shape).astype(BF)


def step_kernel(cfg, names, *refs):
    r = dict(zip(names, refs))
    m, n, nz = cfg["m"], cfg["n"], cfg["n"] // 2
    pds, rows, cols = cfg["pds"], cfg["rows"], cfg["cols"]
    seg = WD * cols
    cells = rows * seg
    half = rows // 2
    hc = cols // 2
    per_row = WD * hc
    few = half * per_row
    fewp = up_to(few, 16)
    hal = up_to(HALO * per_row, 16)
    heads1, heads2, hd = cfg["heads1"], cfg["heads2"], cfg["hd"]
    lanes2 = heads2 * hd
    wins = rows // WL
    lat = lax.axis_index("lat")
    lon = lax.axis_index("lon")
    zi, core = lon // 2, lon % 2
    buddy = lon + 1 - 2 * core
    s0, s1, s2, s3 = r["off"][0], r["off"][1], r["off"][2], r["off"][3]

    def dev(dlat, dlon):
        return (lax.rem(lat + dlat + m, m), lax.rem(lon + dlon + n, n))

    greet = {(0, d) for d in range(1, n)}
    greet |= {(d % m, e) for d in (-1, 1) for e in range(n)}
    greet |= {(d, 0) for d in range(1, m)}
    greet -= {(0, 0)}
    barrier = pltpu.get_barrier_semaphore()
    for dlat, dlon in sorted(greet):
        pl.semaphore_signal(barrier, 1, device_id=dev(dlat, dlon), device_id_type=MESH)

    def local(k, src, dst):
        return pltpu.make_async_copy(src, dst, r["lsem"].at[k])

    E = [r["E%d" % pd] for pd in range(pds)]
    G = [r["G%d" % pd] for pd in range(pds)]
    loads = {
        "x": local(0, r["x"], r["v_x"]),
        "wt": local(2, r["wt"], r["v_wt"]),
        "b1": local(3, r["b1"], r["v_b1"]),
        "wo1": local(4, r["wo1"], r["v_wo1"]),
        "we1": local(5, r["we1"], r["v_we1"]),
        "wr1": local(6, r["wr1"], r["v_wr1"]),
        "mw": local(7, r["mw"], r["v_mw"]),
        "wt2": local(8, r["wt2"], r["v_wt2"].at[core]),
        "b2": local(9, r["b2"], r["v_b2"]),
        "we2": local(10, r["we2"], r["v_we2"].at[core]),
        "wr2": local(11, r["wr2"], r["v_wr2"].at[core]),
        "up": local(12, r["up"], r["v_up"]),
        "wo2": local(13, r["wo2"].at[lat], r["W"].at[core, lat, zi]),
    }
    for key in ("x", "wt", "b1", "wo2"):
        loads[key].start()

    halo_copies = [
        Copies(r["hs%d" % k], r["hr%d" % k], make)
        for k, make in enumerate(
            (
                lambda pd: (E[pd].at[0, pl.ds(0, rows)], E[pd].at[1, pl.ds(0, rows)], dev(0, -1)),
                lambda pd: (E[pd].at[0, pl.ds(0, HALO)], E[pd].at[0, pl.ds(rows, HALO)], dev(-1, 0)),
                lambda pd: (E[pd].at[0, pl.ds(0, HALO)], E[pd].at[1, pl.ds(rows, HALO)], dev(-1, -1)),
            )
        )
    ]
    low = rows - HALO
    back_copies = [
        Copies(r["bs%d" % k], r["br%d" % k], make)
        for k, make in enumerate(
            (
                lambda pd: (G[pd].at[0, pl.ds(HALO, rows)], G[pd].at[1, pl.ds(HALO, rows)], dev(0, 1)),
                lambda pd: (G[pd].at[0, pl.ds(HALO + low, HALO)], G[pd].at[0, pl.ds(0, HALO)], dev(1, 0)),
                lambda pd: (G[pd].at[0, pl.ds(HALO + low, HALO)], G[pd].at[1, pl.ds(0, HALO)], dev(1, 1)),
            )
        )
    ]
    W = r["W"]
    share_lon = Copies(
        r["ws0"], r["wr0"], lambda k: (W.at[core, lat, zi], W.at[core, lat, zi], dev(0, 2 * (k + 1)))
    )
    share_lat = Copies(r["ws1"], r["wr1s"], lambda k: (W.at[core, lat], W.at[core, lat], dev(k + 1, 0)))
    share_core = Copies(r["ws2"], r["wr2s"], lambda k: (W.at[core], W.at[core], (lat, buddy)))

    def swap(k):
        name = ("wt2", "we2", "wr2")[k]
        return pltpu.make_async_remote_copy(
            r[name],
            r["v_" + name].at[core],
            r["ss"].at[k],
            r["sr"].at[k],
            device_id=(lat, buddy),
            device_id_type=MESH,
        )

    X, Y, S, H = r["X"], r["Y"], r["S"], r["H"]

    def relay(buf, sends, recvs):
        def hop(pd, z, way, reach):
            step = 2 - 4 * way
            return pltpu.make_async_remote_copy(
                buf.at[pd, z],
                buf.at[pd, z],
                r[sends].at[pd, way, reach - 1],
                r[recvs].at[pd, way, reach - 1],
                device_id=(lat, lon + step),
                device_id_type=MESH,
            )

        def pass_on(pd, z, way, reach, act):
            @pl.when(jnp.where(way == 0, zi < nz - 1, zi > 0))
            def _():
                act(hop(pd, z, way, reach))

        def start(pd):
            for way in range(2):
                pass_on(pd, zi, way, 1, lambda c: c.start())

        def turn(j):
            both = jnp.minimum(zi, nz - 1 - zi)
            even = j < 2 * both
            way = jnp.where(even, j % 2, jnp.where(zi > nz - 1 - zi, 0, 1))
            reach = jnp.where(even, j // 2 + 1, j - both + 1)
            return zi - reach * (1 - 2 * way), way, reach

        def arrive(pd, j):
            z, way, reach = turn(j)
            hop(pd, z, way, reach).wait_recv()

            @pl.when(reach < nz - 1)
            def _():
                pass_on(pd, z, way, reach + 1, lambda c: c.start())

            return z

        def drain(pd):
            def one(j, carry):
                z, way, reach = turn(j)

                @pl.when(reach < nz - 1)
                def _():
                    pass_on(pd, z, way, reach + 1, lambda c: c.wait_send())

                return carry

            for way in range(2):
                pass_on(pd, zi, way, 1, lambda c: c.wait_send())
            lax.fori_loop(0, nz - 1, one, 0)

        return start, arrive, drain

    gather1_start, gather1_arrive, gather1_drain = relay(X, "as0", "ar0")
    cross = [
        Copies(r["cs%d" % k], r["cr%d" % k], make)
        for k, make in enumerate(
            (
                lambda pd, z: (S.at[pd, z], Y.at[pd, core, z], (lat, buddy)),
                lambda pd, z: (Y.at[pd, core, z, pl.ds(0, hal)], H.at[pd, core, z], dev(-1, 0)),
                lambda pd, z: (S.at[pd, z, pl.ds(0, hal)], H.at[pd, core, z], (lax.rem(lat + m - 1, m), buddy)),
            )
        )
    ]
    C, D, M, N = r["C"], r["D"], r["M"], r["N"]

    def to_owner(pd, k):
        owner = lax.rem(lon + k + 1, n)
        return C.at[pd, owner % 2, owner // 2, pl.ds(0, few)], M.at[pd, lon], (lat, owner)

    def to_next(pd, k):
        owner = lax.rem(lon + k, n)
        return D.at[pd, owner % 2, owner // 2], N.at[pd, lon], (lax.rem(lat + 1, m), owner)

    spread_here = Copies(r["ds0"], r["dr0"], to_owner)
    spread_next = Copies(r["ds1"], r["dr1"], to_next)
    Z, Q, T, R = r["Z"], r["Q"], r["T"], r["R"]
    gather2_start, gather2_arrive, gather2_drain = relay(Z, "as1", "ar1")

    def partial(pd, z):
        way = jnp.where(z > zi, 0, 1)
        step = 2 - 4 * way

        def message(dst, recv, target):
            return pltpu.make_async_remote_copy(
                Q.at[pd, z], dst, r["rs0"].at[pd, z], recv, device_id=(lat, target), device_id_type=MESH
            )

        final = message(T.at[pd, way], r["rr0"].at[pd, way], lon + step)
        between = message(R.at[pd, z], r["rr1"].at[pd, z], lon + step)
        direct = message(T.at[pd, 2], r["rr0"].at[pd, 2], 2 * z + core)
        return jnp.abs(z - zi), final, between, direct

    def partial_start(pd, z):
        reach, final, between, direct = partial(pd, z)

        @pl.when(reach == 1)
        def _():
            final.start()

        straight = nz > 2

        @pl.when((reach > 1) & (reach < (nz - 1 if straight else nz)))
        def _():
            between.start()

        if straight:

            @pl.when(reach == nz - 1)
            def _():
                direct.start()

    def adds(pd, z):
        first = ((z == 0) & (zi == nz - 2)) | ((z == nz - 1) & (zi == 1))
        inner = (zi > 0) & (zi < nz - 1)
        return inner & jnp.logical_not(first)

    def partial_pass(pd, j):
        above, below = nz - 1 - zi, zi
        up = jnp.where(2 * zi < nz, j < above, j >= below)
        z = jnp.where(
            2 * zi < nz,
            jnp.where(up, zi + 1 + j, zi - 1 - (j - above)),
            jnp.where(up, zi + 1 + (j - below), zi - 1 - j),
        )

        @pl.when(adds(pd, z))
        def _():
            partial(pd, z)[2].wait_recv()
            Q[pd, z] = (r["part"][pd, z] + R[pd, z].astype(F32)).astype(BF)
            partial_start(pd, z)

    piece = WL * seg
    q = down(pds * piece)
    inside = q % piece
    to_pairs = one_hot(
        ((inside // seg) * cols + inside % cols) * (pds * WD) + (q // piece) * WD + (inside % seg) // cols,
        along(pds * piece),
    )
    loads["x"].wait()
    for k in range(wins):
        turned = dot32(to_pairs, flat(r["v_x"][k * WL : (k + 1) * WL]))
        for pd in range(pds):
            E[pd][0, k * WL : (k + 1) * WL] = (
                turned[pd * piece : (pd + 1) * piece].reshape(WL, seg, -1).astype(BF)
            )
    pl.semaphore_wait(barrier, len(greet))
    for pd in range(pds):
        for cps in halo_copies:
            cps.one(pd).start()
    loads["wo2"].wait()
    for k in range(nz - 1):
        share_lon.one(k).start()
    for k in range(3):
        swap(k).start()
    for key in ("we2", "wr2", "wt2", "wo1", "we1", "wr1", "mw", "b2", "up"):
        loads[key].start()

    def both_streams(step):
        step(0, 0)

        def pair_of_steps(t, carry):
            step(0, t)
            step(1, t - 1)
            return carry

        lax.fori_loop(1, nz - 1, pair_of_steps, 0)
        step(1, nz - 2)

    def place(index):
        return index // (WL * WW), (index // WW) % WL, index % WW

    a, b, c = place(down(WT))
    q = along(2 * WL * seg)
    r["P1"][...] = one_hot(
        (b * WD + a) * 64 + c + s1,
        ((q % (WL * seg)) // cols) * 64 + (q // (WL * seg)) * cols + q % cols,
    )
    a, b, c = place(along(WT))
    row = down(WT)
    r["U1"][...] = one_hot(row, (b * WD + a) * WW + c)

    ia, j = blocked(down(cells), cells, few, per_row, hc)
    q = along(2 * cells)
    r["B1"][...] = one_hot(
        ia * 64 + j - s1 + cols,
        ((q % cells) // cols) * 64 + jnp.where(q < cells, cols, 0) + q % cols,
    )
    q = along(cells)
    r["B0"][...] = one_hot(ia * cols + j, q)
    def own_key(index, size, first):
        return jnp.where(
            index < size, (index // hc + first * WD) * 64 + index % hc, -1
        )

    a, b, c = place(down(WT))
    q = along(4 * fewp + 4 * hal)
    far = q >= 4 * fewp
    qh = q - 4 * fewp
    chunk = jnp.where(far, qh // hal, q // fewp)
    key = jnp.where(far, own_key(qh % hal, HALO * per_row, half), own_key(q % fewp, few, 0))
    r["P2"][...] = one_hot(
        ((b + s2) * WD + a) * 64 + c + s3, jnp.where(key < 0, -1, key + chunk * hc)
    )
    a, b, c = place(along(2 * WT) % WT)
    x = c + s3 - jnp.where(along(2 * WT) < WT, 0, cols)
    col_key = jnp.where((x >= 0) & (x < cols), ((b + s2) * WD + a) * 64 + x, -2)
    q = down(2 * fewp + 2 * hal)
    far = q >= 2 * fewp
    qh = q - 2 * fewp
    chunk = jnp.where(far, qh // hal, q // fewp)
    key = jnp.where(far, own_key(qh % hal, HALO * per_row, half), own_key(q % fewp, few, 0))
    r["U2"][...] = one_hot(jnp.where(key < 0, -1, key + chunk * hc), col_key)

    pad = jnp.zeros((fewp - few, 3 * lanes2), BF)
    for pd in range(pds):
        for z in range(nz):
            S[pd, z, few:] = pad
    for k in range(wins):
        r["K1"][k] = window_mask(rows * m - s0 - lat * rows - k * WL)
    r["K2"][...] = window_mask(half * m - s2 - lat * half)

    group = 4 if heads1 % 4 == 0 else heads1
    width = 3 * group * hd
    loads["wt"].wait()
    order = head_order(group, hd)
    for g in range(heads1 // group):
        cut = slice(g * width, (g + 1) * width)
        r["wt_o"][:, cut] = dot32(r["v_wt"][:, cut], order).astype(BF)
    for pd in range(pds):
        r["F"][pd] = dot32(r["B0"][...], flat(E[pd][0, :rows])).astype(BF)
    loads["b1"].wait()

    def fine_attention(pd):
        for cps in halo_copies:
            cps.one(pd).wait_recv()
        for k in range(wins):
            near = flat(E[pd][:, pl.ds(s0 + k * WL, WL)])
            framed = dot32(r["P1"][...], near)
            r["A"][pl.ds(k * WT, WT), :] = layer_norm(framed, r["g1"][...])
        r["tri"][...] = dot32(r["A"][...], r["wt_o"][...]).astype(BF)

        def one_group(g, carry):
            for k in range(wins):
                part = r["tri"][pl.ds(k * WT, WT), pl.ds(pl.multiple_of(g * width, 128), width)]
                total = attend(part, group, hd, lambda h: r["v_b1"][g * group + h], r["K1"][k])
                r["A"][pl.ds(k * WT, WT), pl.ds(pl.multiple_of(g * group * hd, 128), group * hd)] = (
                    total.astype(BF)
                )
            return carry

        lax.fori_loop(0, heads1 // group, one_group, 0)
        for k in range(wins):
            turned = dot32(r["U1"][...], r["A"][pl.ds(k * WT, WT), :])
            G[pd][0, pl.ds(HALO + k * WL, WL)] = turned.reshape(WL, seg, -1).astype(BF)
        for cps in back_copies:
            cps.one(pd).start()

    for pd in range(pds):
        fine_attention(pd)

    for k in range(nz - 1):
        share_lon.one(k).wait_recv()
    for k in range(m - 1):
        share_lat.one(k).start()
    loads["wt2"].wait()
    swap(0).wait_recv()
    order = head_order(heads2, hd)
    for k in range(2):
        r["wt2_o"][k] = dot32(r["v_wt2"][k], order).astype(BF)
    for key in ("wo1", "we1", "wr1", "mw"):
        loads[key].wait()

    def fine_tail(pd):
        for cps in back_copies:
            cps.one(pd).wait_recv()
        r["near"][...] = flat(G[pd][:, pl.ds(HALO - s0, rows)])

        def some_rows(k, carry):
            at = pl.ds(pl.multiple_of(k * (cells // 2), 16), cells // 2)
            mixed = dot32(r["B1"][at, :], r["near"][...]).astype(BF)
            attended = (r["F"][pd, at, :].astype(F32) + dot32(mixed, r["v_wo1"][...])).astype(BF)
            normed = layer_norm(attended, r["gm"][...])
            hidden = jax.nn.gelu(dot32(normed, r["v_we1"][...])).astype(BF)
            state = (attended.astype(F32) + dot32(hidden, r["v_wr1"][...])).astype(BF)
            r["state"][pd, at, :] = state.astype(F32)
            return carry

        lax.fori_loop(0, 2, some_rows, 0)
        merged = jnp.concatenate([r["state"][pd, k * few : (k + 1) * few, :] for k in range(4)], axis=1)
        coarse_in = dot32(layer_norm(merged, r["mg"][...]), r["v_mw"][...]).astype(BF)
        r["cin"][pd] = coarse_in
        X[pd, zi] = layer_norm(coarse_in, r["g2"][...])
        gather1_start(pd)

    for pd in range(pds):
        fine_tail(pd)

    for pd in range(pds):
        for z in range(nz):
            Y[pd, core, z, few:] = pad

    def project(pd, z):
        given = X[pd, z]
        S[pd, z, pl.ds(0, few)] = dot32(given, r["wt2_o"][1 - core]).astype(BF)
        cross[0].one(pd, z).start()
        cross[2].one(pd, z).start()
        Y[pd, core, z, pl.ds(0, few)] = dot32(given, r["wt2_o"][core]).astype(BF)
        cross[1].one(pd, z).start()

    for pd in range(pds):
        project(pd, zi)
    both_streams(lambda pd, j: project(pd, gather1_arrive(pd, j)))
    for k in range(m - 1):
        share_lat.one(k).wait_recv()
    share_core.one(0).start()
    loads["b2"].wait()

    def coarse_attention(pd, carry):
        for z in range(nz):
            for cps in cross:
                cps.one(pd, z).wait_recv()

        def one_window(w, carry):
            zs = [lax.rem(w + dz, nz) for dz in range(2)]
            pieces = [Y[pd, par, z] for z in zs for par in range(2)]
            pieces += [H[pd, par, z] for z in zs for par in range(2)]
            part = dot32(r["P2"][...], jnp.concatenate(pieces, axis=0))
            total = attend(part, heads2, hd, lambda h: r["v_b2"][h], r["K2"][...])
            r["V"][w] = total.astype(BF)
            return carry

        lax.fori_loop(0, nz, one_window, 0)

        def one_chip(z, carry):
            both = jnp.concatenate([r["V"][z], r["V"][lax.rem(z + nz - 1, nz)]], axis=0)
            back = dot32(r["U2"][...], both).astype(BF)
            for par in range(2):
                C[pd, par, z] = back[par * fewp : (par + 1) * fewp]
                D[pd, par, z] = back[2 * fewp + par * hal : 2 * fewp + (par + 1) * hal]
            return carry

        lax.fori_loop(0, nz, one_chip, 0)
        for k in range(n - 1):
            spread_here.one(pd, k).start()
        for k in range(n):
            spread_next.one(pd, k).start()
        M[pd, lon] = C[pd, core, zi, pl.ds(0, few)]
        return carry

    coarse_attention(0, 0)
    coarse_attention(1, 0)
    share_core.one(0).wait_recv()

    def coarse_output(pd, carry):
        for k in range(n - 1):
            spread_here.one(pd, k).wait_recv()
        for k in range(n):
            spread_next.one(pd, k).wait_recv()
        value = r["cin"][pd].astype(F32)
        tail = jnp.zeros((few - hal, lanes2), F32)
        for g in range(n):
            part = M[pd, g].astype(F32) + jnp.concatenate([N[pd, g].astype(F32), tail], axis=0)
            rows_g = W[g % 2, :, g // 2]
            rows_g = rows_g.reshape(lanes2, -1) if rows_g.shape[1] % 16 == 0 else flat(rows_g)
            value += dot32(part.astype(BF), rows_g)
        middle = value.astype(BF)
        r["mid"][pd] = middle
        Z[pd, zi] = layer_norm(middle, r["gm2"][...])
        gather2_start(pd)
        return carry

    coarse_output(0, 0)
    coarse_output(1, 0)
    for key in ("we2", "wr2", "up"):
        loads[key].wait()
    swap(1).wait_recv()
    swap(2).wait_recv()

    def feed(pd, z):
        given = Z[pd, z]
        total = None
        for k in range(2):
            hidden = jax.nn.gelu(dot32(given, r["v_we2"][k])).astype(BF)
            term = dot32(hidden, r["v_wr2"][k])
            total = term if total is None else total + term
        return total

    def feed_step(pd, j):
        z = gather2_arrive(pd, j)
        term = feed(pd, z)

        @pl.when(adds(pd, z))
        def _():
            r["part"][pd, z] = term

        @pl.when(jnp.logical_not(adds(pd, z)))
        def _():
            Q[pd, z] = term.astype(BF)
            partial_start(pd, z)

    for pd in range(pds):
        r["own"][pd] = feed(pd, zi)
    both_streams(feed_step)
    for pd in range(pds):

        def pass_one(j, carry):
            partial_pass(pd, j)
            return carry

        lax.fori_loop(0, nz - 1, pass_one, 0)

    def finish(pd):
        r["sum"][...] = r["mid"][pd].astype(F32) + r["own"][pd]
        for way in range(3 if nz > 2 else 2):
            end = (zi == 0) | (zi == nz - 1)

            @pl.when((zi > 0, zi < nz - 1, end)[way])
            def _():
                pltpu.make_async_remote_copy(
                    Q.at[pd, zi],
                    T.at[pd, way],
                    r["rs0"].at[pd, zi],
                    r["rr0"].at[pd, way],
                    device_id=(lat, buddy),
                    device_id_type=MESH,
                ).wait_recv()
                r["sum"][...] = r["sum"][...] + T[pd, way].astype(F32)

        value = r["sum"][...]
        state = value.astype(BF)
        r["cstate"][pd] = state
        expanded = dot32(state, r["v_up"][...])
        channels = expanded.shape[1] // 4
        for k in range(4):
            at = slice(k * few, (k + 1) * few)
            cut = slice(k * channels, (k + 1) * channels)
            r["blended"][pd, at, :] = (r["state"][pd, at, :] + expanded[:, cut]).astype(BF)

    for pd in range(pds):
        finish(pd)

    for pd in range(pds):
        for cps in halo_copies + back_copies:
            cps.one(pd).wait_send()
        for z in range(nz):
            for cps in cross:
                cps.one(pd, z).wait_send()
        gather1_drain(pd)
        gather2_drain(pd)
        for k in range(1, nz):
            partial(pd, lax.rem(zi + k, nz))[1].wait_send()
        for k in range(n - 1):
            spread_here.one(pd, k).wait_send()
        for k in range(n):
            spread_next.one(pd, k).wait_send()
    for k in range(nz - 1):
        share_lon.one(k).wait_send()
    for k in range(m - 1):
        share_lat.one(k).wait_send()
    share_core.one(0).wait_send()
    for k in range(3):
        swap(k).wait_send()


def body(
    fine_field,
    offsets,
    fine_prenorm,
    fine_triple,
    fine_bias,
    fine_output,
    fine_midnorm,
    fine_expand,
    fine_reduce,
    merge_gain,
    merge_weight,
    coarse_prenorm,
    coarse_triple,
    coarse_bias,
    coarse_output,
    coarse_midnorm,
    coarse_expand,
    coarse_reduce,
    upsample_weight,
):
    levels, rows, cols, channels = fine_field.shape
    m = lax.axis_size("lat")
    n = lax.axis_size("lon")
    nz = n // 2
    pds = levels // WD
    wide = coarse_output.shape[1]
    heads1, heads2 = fine_bias.shape[0], coarse_bias.shape[0]
    hd = channels // heads1
    lanes2 = coarse_output.shape[0]
    assert cols == WW and rows == 2 * WL and n % 2 == 0 and nz >= 2 and pds == 2
    assert lanes2 == heads2 * hd and lanes2 % m == 0
    half, hc = rows // 2, cols // 2
    seg = WD * cols
    cells = rows * seg
    few = cells // 4
    fewp = up_to(few, 16)
    hal = up_to(HALO * WD * hc, 16)

    x = fine_field.transpose(1, 2, 0, 3)
    vmem = pl.BlockSpec(memory_space=pltpu.VMEM)
    hbm = pl.BlockSpec(memory_space=pl.ANY)
    args = [
        ("off", offsets, pl.BlockSpec(memory_space=pltpu.SMEM)),
        ("x", x, hbm),
        ("g1", fine_prenorm[None], vmem),
        ("wt", fine_triple, hbm),
        ("b1", fine_bias, hbm),
        ("wo1", fine_output, hbm),
        ("gm", fine_midnorm[None], vmem),
        ("we1", fine_expand, hbm),
        ("wr1", fine_reduce, hbm),
        ("mg", merge_gain[None], vmem),
        ("mw", merge_weight, hbm),
        ("g2", coarse_prenorm[None], vmem),
        ("wt2", coarse_triple, hbm),
        ("b2", coarse_bias, hbm),
        ("wo2", coarse_output.reshape(m, lanes2 // m, wide), hbm),
        ("gm2", coarse_midnorm[None], vmem),
        ("we2", coarse_expand, hbm),
        ("wr2", coarse_reduce, hbm),
        ("up", upsample_weight, hbm),
    ]
    outs = [
        ("blended", jax.ShapeDtypeStruct((pds, cells, channels), BF)),
        ("cstate", jax.ShapeDtypeStruct((pds, few, wide), BF)),
    ]
    sem = pltpu.SemaphoreType.DMA
    wide3 = 3 * lanes2
    scratch = [
        ("lsem", sem((14,))),
        ("v_wt", pltpu.VMEM(fine_triple.shape, BF)),
        ("wt_o", pltpu.VMEM(fine_triple.shape, BF)),
        ("v_b1", pltpu.VMEM(fine_bias.shape, F32)),
        ("v_wo1", pltpu.VMEM(fine_output.shape, BF)),
        ("v_we1", pltpu.VMEM(fine_expand.shape, BF)),
        ("v_wr1", pltpu.VMEM(fine_reduce.shape, BF)),
        ("v_mw", pltpu.VMEM(merge_weight.shape, BF)),
        ("v_wt2", pltpu.VMEM((2,) + coarse_triple.shape, BF)),
        ("wt2_o", pltpu.VMEM((2,) + coarse_triple.shape, BF)),
        ("v_b2", pltpu.VMEM(coarse_bias.shape, F32)),
        ("v_we2", pltpu.VMEM((2,) + coarse_expand.shape, BF)),
        ("v_wr2", pltpu.VMEM((2,) + coarse_reduce.shape, BF)),
        ("v_up", pltpu.VMEM(upsample_weight.shape, BF)),
        ("W", pltpu.VMEM((2, m, nz, lanes2 // m, wide), BF)),
        ("P1", pltpu.VMEM((WT, 2 * WL * seg), BF)),
        ("U1", pltpu.VMEM((WT, WT), BF)),
        ("B0", pltpu.VMEM((cells, cells), BF)),
        ("B1", pltpu.VMEM((cells, 2 * cells), BF)),
        ("v_x", pltpu.VMEM(x.shape, BF)),
        ("P2", pltpu.VMEM((WT, 4 * fewp + 4 * hal), BF)),
        ("U2", pltpu.VMEM((2 * fewp + 2 * hal, 2 * WT), BF)),
        ("K1", pltpu.VMEM((rows // WL, WT, WT), F32)),
        ("K2", pltpu.VMEM((WT, WT), F32)),
        ("F", pltpu.VMEM((pds, cells, channels), BF)),
        ("A", pltpu.VMEM((cells, channels), BF)),
        ("tri", pltpu.VMEM((cells, 3 * channels), BF)),
        ("near", pltpu.VMEM((2 * cells, channels), BF)),
        ("state", pltpu.VMEM((pds, cells, channels), F32)),
        ("cin", pltpu.VMEM((pds, few, wide), BF)),
        ("X", pltpu.VMEM((pds, nz, few, wide), BF)),
        ("Y", pltpu.VMEM((pds, 2, nz, fewp, wide3), BF)),
        ("S", pltpu.VMEM((pds, nz, fewp, wide3), BF)),
        ("H", pltpu.VMEM((pds, 2, nz, hal, wide3), BF)),
        ("V", pltpu.VMEM((nz, WT, lanes2), BF)),
        ("C", pltpu.VMEM((pds, 2, nz, fewp, lanes2), BF)),
        ("D", pltpu.VMEM((pds, 2, nz, hal, lanes2), BF)),
        ("M", pltpu.VMEM((pds, n, few, lanes2), BF)),
        ("N", pltpu.VMEM((pds, n, hal, lanes2), BF)),
        ("mid", pltpu.VMEM((pds, few, wide), BF)),
        ("Z", pltpu.VMEM((pds, nz, few, wide), BF)),
        ("own", pltpu.VMEM((pds, few, wide), F32)),
        ("Q", pltpu.VMEM((pds, nz, few, wide), BF)),
        ("T", pltpu.VMEM((pds, 3, few, wide), BF)),
        ("R", pltpu.VMEM((pds, nz, few, wide), BF)),
        ("part", pltpu.VMEM((pds, nz, few, wide), F32)),
        ("sum", pltpu.VMEM((few, wide), F32)),
    ]
    for pd in range(pds):
        for name in ("E", "G"):
            scratch.append((name + str(pd), pltpu.VMEM((2, rows + HALO, seg, channels), BF)))
    for name, shape in (("h", (pds,)), ("b", (pds,)), ("c", (pds, nz))):
        for k in range(3):
            scratch += [("%ss%d" % (name, k), sem(shape)), ("%sr%d" % (name, k), sem(shape))]
    for s, d, shape in (
        ("ws0", "wr0", (nz - 1,)),
        ("ws1", "wr1s", (m - 1,)),
        ("ws2", "wr2s", (1,)),
        ("ss", "sr", (3,)),
        ("as0", "ar0", (pds, 2, nz - 1)),
        ("as1", "ar1", (pds, 2, nz - 1)),
        ("ds0", "dr0", (pds, n - 1)),
        ("ds1", "dr1", (pds, n)),
    ):
        scratch += [(s, sem(shape)), (d, sem(shape))]
    scratch += [("rs0", sem((pds, nz))), ("rr0", sem((pds, 3))), ("rr1", sem((pds, nz)))]

    cfg = dict(m=m, n=n, pds=pds, rows=rows, cols=cols, heads1=heads1, heads2=heads2, hd=hd)
    names = [a[0] for a in args] + [o[0] for o in outs] + [s[0] for s in scratch]
    blended, state = pl.pallas_call(
        functools.partial(step_kernel, cfg, names),
        out_shape=[o[1] for o in outs],
        in_specs=[a[2] for a in args],
        out_specs=[vmem, vmem],
        scratch_shapes=[s[1] for s in scratch],
        compiler_params=pltpu.CompilerParams(
            collective_id=0, has_side_effects=True, vmem_limit_bytes=63 << 20
        ),
    )(*[a[1] for a in args])
    blended, state = pl.pallas_call(
        arrange_kernel,
        out_shape=[
            jax.ShapeDtypeStruct(x.shape, BF),
            jax.ShapeDtypeStruct((half, hc, levels, wide), BF),
        ],
        in_specs=[vmem, vmem],
        out_specs=[vmem, vmem],
    )(blended, state)
    return blended.transpose(2, 0, 1, 3), state.transpose(2, 0, 1, 3)


def solution(mesh):
    placed = (
        P(None, "lat", "lon", None),
        P(),
        P(),
        P(),
        P(),
        P(),
        P(),
        P(),
        P(),
        P(),
        P(),
        P(),
        P(None, "lon"),
        P("lon", None, None),
        P("lon", None),
        P(),
        P(None, "lon"),
        P("lon", None),
        P(),
    )
    return jax.shard_map(
        body,
        mesh=mesh,
        in_specs=placed,
        out_specs=(P(None, "lat", "lon", None), P(None, "lat", "lon", None)),
        check_vma=False,
    )
```

```python
import functools

import jax
import jax.numpy as jnp
from jax import lax
from jax.experimental import pallas as pl
from jax.experimental.pallas import tpu as pltpu
from jax.sharding import PartitionSpec as P

WD = 2
WL = 6
WW = 12
WT = 144
HALO = WL - 1

epsilon = 1e-05
masked_score = -1e30
BF = jnp.bfloat16
F32 = jnp.float32
I32 = jnp.int32
MESH = pl.DeviceIdType.MESH


def up_to(value, step):
    return -(-value // step) * step


def layer_norm(values, gain_vec):
    values = values.astype(F32)
    center = jnp.mean(values, axis=-1, keepdims=True)
    offset_vals = values - center
    spread = jnp.mean(offset_vals * offset_vals, axis=-1, keepdims=True)
    return (offset_vals * lax.rsqrt(spread + epsilon) * gain_vec).astype(BF)


def dot32(left, right):
    return jnp.dot(left, right, preferred_element_type=F32)


def down(count):
    return lax.broadcasted_iota(I32, (count, 1), 0)


def along(count):
    return lax.broadcasted_iota(I32, (1, count), 1)


def one_hot(row_key, col_key):
    return (row_key == col_key).astype(F32).astype(BF)


def flat(block):
    return block.astype(F32).reshape(-1, block.shape[-1]).astype(BF)


def window_mask(limit):
    row = (lax.broadcasted_iota(I32, (WT, WT), 0) // WW) % WL
    col = (lax.broadcasted_iota(I32, (WT, WT), 1) // WW) % WL
    row_in = (row >= limit).astype(I32)
    col_in = (col >= limit).astype(I32)
    return jnp.where(row_in == col_in, 0.0, masked_score)


def head_order(heads, head_dim):
    lanes = heads * head_dim
    width = 3 * lanes
    row = down(width)
    col = along(width)
    origin = ((col % lanes) // head_dim) * (3 * head_dim) + (col // lanes) * head_dim + col % head_dim
    return one_hot(row, origin)


def attend(part, heads, head_dim, bias_at, place_mask):
    lanes = heads * head_dim
    queries = part[:, :lanes].astype(F32)
    keys_all = part[:, lanes : 2 * lanes].astype(BF)
    values = part[:, 2 * lanes :].astype(BF)
    lane = lax.broadcasted_iota(I32, (WT, lanes), 1) // head_dim
    total = None
    for h in range(heads):
        mine = jnp.where(lane == h, queries, 0.0).astype(BF)
        scores = lax.dot_general(
            mine, keys_all, (((1,), (1,)), ((), ())), preferred_element_type=F32
        )
        scores = scores * head_dim ** (-0.5) + bias_at(h) + place_mask
        top = jnp.max(scores, axis=-1, keepdims=True)
        lifted = jnp.exp(scores - top)
        weight_sum = jnp.sum(lifted, axis=-1, keepdims=True)
        mixed = dot32(lifted.astype(BF), values) / weight_sum
        mixed = jnp.where(lane == h, mixed, 0.0)
        total = mixed if total is None else total + mixed
    return total


class Copies:
    def __init__(self, send, recv, make):
        self.send, self.recv, self.make = send, recv, make

    def one(self, *index):
        src, dst, device = self.make(*index)
        return pltpu.make_async_remote_copy(
            src, dst, self.send.at[index], self.recv.at[index], device_id=device, device_id_type=MESH
        )


def blocked(index, cells, few, per_row, hc):
    block, cell = index // few, index % few
    i = (cell // per_row) * 2 + block % 2
    j = (cell % hc) * 2 + block // 2
    return i * WD + (cell // hc) % WD, j


def arrange_kernel(fine_ref, coarse_ref, fine_out, coarse_out):
    pds, cells, _ = fine_ref.shape
    few = coarse_ref.shape[1]
    _, cols, levels, _ = fine_out.shape
    hc = cols // 2
    per_row = WD * hc
    q = along(pds * cells)
    ia, j = blocked(q % cells, cells, few, per_row, hc)
    chosen = one_hot(down(pds * cells), ((ia // WD) * cols + j) * levels + (q // cells) * WD + ia % WD)
    fine_out[...] = dot32(chosen, flat(fine_ref[...])).reshape(fine_out.shape).astype(BF)
    q = along(pds * few)
    cell = q % few
    chosen = one_hot(
        down(pds * few),
        ((cell // per_row) * hc + cell % hc) * levels + (q // few) * WD + (cell // hc) % WD,
    )
    coarse_out[...] = dot32(chosen, flat(coarse_ref[...])).reshape(coarse_out.shape).astype(BF)


def step_kernel(cfg, names, *refs):
    r = dict(zip(names, refs))
    m, n, nz = cfg["m"], cfg["n"], cfg["n"] // 2
    pds, rows, cols = cfg["pds"], cfg["rows"], cfg["cols"]
    seg = WD * cols
    cells = rows * seg
    half = rows // 2
    hc = cols // 2
    per_row = WD * hc
    few = half * per_row
    fewp = up_to(few, 16)
    hal = up_to(HALO * per_row, 16)
    heads1, heads2, hd = cfg["heads1"], cfg["heads2"], cfg["hd"]
    lanes2 = heads2 * hd
    wins = rows // WL
    lat = lax.axis_index("lat")
    lon = lax.axis_index("lon")
    zi, core = lon // 2, lon % 2
    buddy = lon + 1 - 2 * core
    s0, s1, s2, s3 = r["off"][0], r["off"][1], r["off"][2], r["off"][3]

    def dev(dlat, dlon):
        return (lax.rem(lat + dlat + m, m), lax.rem(lon + dlon + n, n))

    greet = {(0, d) for d in range(1, n)}
    greet |= {(d % m, e) for d in (-1, 1) for e in range(n)}
    greet |= {(d, 0) for d in range(1, m)}
    greet -= {(0, 0)}
    barrier = pltpu.get_barrier_semaphore()
    for dlat, dlon in sorted(greet):
        pl.semaphore_signal(barrier, 1, device_id=dev(dlat, dlon), device_id_type=MESH)

    def local(k, src, dst):
        return pltpu.make_async_copy(src, dst, r["lsem"].at[k])

    E = [r["E%d" % pd] for pd in range(pds)]
    G = [r["G%d" % pd] for pd in range(pds)]
    loads = {
        "x": local(0, r["x"], r["v_x"]),
        "wt": local(2, r["wt"], r["v_wt"]),
        "b1": local(3, r["b1"], r["v_b1"]),
        "wo1": local(4, r["wo1"], r["v_wo1"]),
        "we1": local(5, r["we1"], r["v_we1"]),
        "wr1": local(6, r["wr1"], r["v_wr1"]),
        "mw": local(7, r["mw"], r["v_mw"]),
        "wt2": local(8, r["wt2"], r["v_wt2"].at[core]),
        "b2": local(9, r["b2"], r["v_b2"]),
        "we2": local(10, r["we2"], r["v_we2"].at[core]),
        "wr2": local(11, r["wr2"], r["v_wr2"].at[core]),
        "up": local(12, r["up"], r["v_up"]),
        "wo2": local(13, r["wo2"].at[lat], r["W"].at[core, lat, zi]),
    }
    for key in ("x", "wt", "b1", "wo2"):
        loads[key].start()

    halo_copies = [
        Copies(r["hs%d" % k], r["hr%d" % k], make)
        for k, make in enumerate(
            (
                lambda pd: (E[pd].at[0, pl.ds(0, rows)], E[pd].at[1, pl.ds(0, rows)], dev(0, -1)),
                lambda pd: (E[pd].at[0, pl.ds(0, HALO)], E[pd].at[0, pl.ds(rows, HALO)], dev(-1, 0)),
                lambda pd: (E[pd].at[0, pl.ds(0, HALO)], E[pd].at[1, pl.ds(rows, HALO)], dev(-1, -1)),
            )
        )
    ]
    low = rows - HALO
    back_copies = [
        Copies(r["bs%d" % k], r["br%d" % k], make)
        for k, make in enumerate(
            (
                lambda pd: (G[pd].at[0, pl.ds(HALO, rows)], G[pd].at[1, pl.ds(HALO, rows)], dev(0, 1)),
                lambda pd: (G[pd].at[0, pl.ds(HALO + low, HALO)], G[pd].at[0, pl.ds(0, HALO)], dev(1, 0)),
                lambda pd: (G[pd].at[0, pl.ds(HALO + low, HALO)], G[pd].at[1, pl.ds(0, HALO)], dev(1, 1)),
            )
        )
    ]
    W = r["W"]
    share_lon = Copies(
        r["ws0"], r["wr0"], lambda k: (W.at[core, lat, zi], W.at[core, lat, zi], dev(0, 2 * (k + 1)))
    )
    share_lat = Copies(r["ws1"], r["wr1s"], lambda k: (W.at[core, lat], W.at[core, lat], dev(k + 1, 0)))
    share_core = Copies(r["ws2"], r["wr2s"], lambda k: (W.at[core], W.at[core], (lat, buddy)))

    def swap(k):
        name = ("wt2", "we2", "wr2")[k]
        return pltpu.make_async_remote_copy(
            r[name],
            r["v_" + name].at[core],
            r["ss"].at[k],
            r["sr"].at[k],
            device_id=(lat, buddy),
            device_id_type=MESH,
        )

    X, Y, S, H = r["X"], r["Y"], r["S"], r["H"]

    def relay(buf, sends, recvs):
        def hop(pd, z, way, reach):
            step = 2 - 4 * way
            return pltpu.make_async_remote_copy(
                buf.at[pd, z],
                buf.at[pd, z],
                r[sends].at[pd, way, reach - 1],
                r[recvs].at[pd, way, reach - 1],
                device_id=(lat, lon + step),
                device_id_type=MESH,
            )

        def pass_on(pd, z, way, reach, act):
            @pl.when(jnp.where(way == 0, zi < nz - 1, zi > 0))
            def _():
                act(hop(pd, z, way, reach))

        def start(pd):
            for way in range(2):
                pass_on(pd, zi, way, 1, lambda c: c.start())

        def turn(j):
            both = jnp.minimum(zi, nz - 1 - zi)
            even = j < 2 * both
            way = jnp.where(even, j % 2, jnp.where(zi > nz - 1 - zi, 0, 1))
            reach = jnp.where(even, j // 2 + 1, j - both + 1)
            return zi - reach * (1 - 2 * way), way, reach

        def arrive(pd, j):
            z, way, reach = turn(j)
            hop(pd, z, way, reach).wait_recv()

            @pl.when(reach < nz - 1)
            def _():
                pass_on(pd, z, way, reach + 1, lambda c: c.start())

            return z

        def drain(pd):
            def one(j, carry):
                z, way, reach = turn(j)

                @pl.when(reach < nz - 1)
                def _():
                    pass_on(pd, z, way, reach + 1, lambda c: c.wait_send())

                return carry

            for way in range(2):
                pass_on(pd, zi, way, 1, lambda c: c.wait_send())
            lax.fori_loop(0, nz - 1, one, 0)

        return start, arrive, drain

    gather1_start, gather1_arrive, gather1_drain = relay(X, "as0", "ar0")
    cross = [
        Copies(r["cs%d" % k], r["cr%d" % k], make)
        for k, make in enumerate(
            (
                lambda pd, z: (S.at[pd, z], Y.at[pd, core, z], (lat, buddy)),
                lambda pd, z: (Y.at[pd, core, z, pl.ds(0, hal)], H.at[pd, core, z], dev(-1, 0)),
                lambda pd, z: (S.at[pd, z, pl.ds(0, hal)], H.at[pd, core, z], (lax.rem(lat + m - 1, m), buddy)),
            )
        )
    ]
    C, D, M, N = r["C"], r["D"], r["M"], r["N"]

    def to_owner(pd, k):
        owner = lax.rem(lon + k + 1, n)
        return C.at[pd, owner % 2, owner // 2, pl.ds(0, few)], M.at[pd, lon], (lat, owner)

    def to_next(pd, k):
        owner = lax.rem(lon + k, n)
        return D.at[pd, owner % 2, owner // 2], N.at[pd, lon], (lax.rem(lat + 1, m), owner)

    spread_here = Copies(r["ds0"], r["dr0"], to_owner)
    spread_next = Copies(r["ds1"], r["dr1"], to_next)
    Z, Q, T, R = r["Z"], r["Q"], r["T"], r["R"]
    gather2_start, gather2_arrive, gather2_drain = relay(Z, "as1", "ar1")

    def partial(pd, z):
        way = jnp.where(z > zi, 0, 1)
        step = 2 - 4 * way

        def message(dst, recv, target):
            return pltpu.make_async_remote_copy(
                Q.at[pd, z], dst, r["rs0"].at[pd, z], recv, device_id=(lat, target), device_id_type=MESH
            )

        final = message(T.at[pd, way], r["rr0"].at[pd, way], lon + step)
        between = message(R.at[pd, z], r["rr1"].at[pd, z], lon + step)
        direct = message(T.at[pd, 2], r["rr0"].at[pd, 2], 2 * z + core)
        return jnp.abs(z - zi), final, between, direct

    def partial_start(pd, z):
        reach, final, between, direct = partial(pd, z)

        @pl.when(reach == 1)
        def _():
            final.start()

        straight = nz > 2

        @pl.when((reach > 1) & (reach < (nz - 1 if straight else nz)))
        def _():
            between.start()

        if straight:

            @pl.when(reach == nz - 1)
            def _():
                direct.start()

    def adds(pd, z):
        first = ((z == 0) & (zi == nz - 2)) | ((z == nz - 1) & (zi == 1))
        inner = (zi > 0) & (zi < nz - 1)
        return inner & jnp.logical_not(first)

    def partial_pass(pd, j):
        above, below = nz - 1 - zi, zi
        up = jnp.where(2 * zi < nz, j < above, j >= below)
        z = jnp.where(
            2 * zi < nz,
            jnp.where(up, zi + 1 + j, zi - 1 - (j - above)),
            jnp.where(up, zi + 1 + (j - below), zi - 1 - j),
        )

        @pl.when(adds(pd, z))
        def _():
            partial(pd, z)[2].wait_recv()
            Q[pd, z] = (r["part"][pd, z] + R[pd, z].astype(F32)).astype(BF)
            partial_start(pd, z)

    piece = WL * seg
    q = down(pds * piece)
    inside = q % piece
    to_pairs = one_hot(
        ((inside // seg) * cols + inside % cols) * (pds * WD) + (q // piece) * WD + (inside % seg) // cols,
        along(pds * piece),
    )
    loads["x"].wait()
    for k in range(wins):
        turned = dot32(to_pairs, flat(r["v_x"][k * WL : (k + 1) * WL]))
        for pd in range(pds):
            E[pd][0, k * WL : (k + 1) * WL] = (
                turned[pd * piece : (pd + 1) * piece].reshape(WL, seg, -1).astype(BF)
            )
    pl.semaphore_wait(barrier, len(greet))
    for pd in range(pds):
        for cps in halo_copies[::-1]:
            cps.one(pd).start()
    loads["wo2"].wait()
    for k in range(nz - 1):
        share_lon.one(k).start()
    for k in range(3):
        swap(k).start()
    for key in ("we2", "wr2", "wt2", "wo1", "we1", "wr1", "mw", "b2", "up"):
        loads[key].start()

    def both_streams(step):
        step(0, 0)

        def pair_of_steps(t, carry):
            step(0, t)
            step(1, t - 1)
            return carry

        lax.fori_loop(1, nz - 1, pair_of_steps, 0)
        step(1, nz - 2)

    def place(index):
        return index // (WL * WW), (index // WW) % WL, index % WW

    a, b, c = place(down(WT))
    q = along(2 * WL * seg)
    r["P1"][...] = one_hot(
        (b * WD + a) * 64 + c + s1,
        ((q % (WL * seg)) // cols) * 64 + (q // (WL * seg)) * cols + q % cols,
    )
    a, b, c = place(along(WT))
    row = down(WT)
    r["U1"][...] = one_hot(row, (b * WD + a) * WW + c)

    ia, j = blocked(down(cells), cells, few, per_row, hc)
    q = along(2 * cells)
    r["B1"][...] = one_hot(
        ia * 64 + j - s1 + cols,
        ((q % cells) // cols) * 64 + jnp.where(q < cells, cols, 0) + q % cols,
    )
    q = along(cells)
    r["B0"][...] = one_hot(ia * cols + j, q)
    def own_key(index, size, first):
        return jnp.where(
            index < size, (index // hc + first * WD) * 64 + index % hc, -1
        )

    a, b, c = place(down(WT))
    q = along(4 * fewp + 4 * hal)
    far = q >= 4 * fewp
    qh = q - 4 * fewp
    chunk = jnp.where(far, qh // hal, q // fewp)
    key = jnp.where(far, own_key(qh % hal, HALO * per_row, half), own_key(q % fewp, few, 0))
    r["P2"][...] = one_hot(
        ((b + s2) * WD + a) * 64 + c + s3, jnp.where(key < 0, -1, key + chunk * hc)
    )
    a, b, c = place(along(2 * WT) % WT)
    x = c + s3 - jnp.where(along(2 * WT) < WT, 0, cols)
    col_key = jnp.where((x >= 0) & (x < cols), ((b + s2) * WD + a) * 64 + x, -2)
    q = down(2 * fewp + 2 * hal)
    far = q >= 2 * fewp
    qh = q - 2 * fewp
    chunk = jnp.where(far, qh // hal, q // fewp)
    key = jnp.where(far, own_key(qh % hal, HALO * per_row, half), own_key(q % fewp, few, 0))
    r["U2"][...] = one_hot(jnp.where(key < 0, -1, key + chunk * hc), col_key)

    pad = jnp.zeros((fewp - few, 3 * lanes2), BF)
    for pd in range(pds):
        for z in range(nz):
            S[pd, z, few:] = pad
    for k in range(wins):
        r["K1"][k] = window_mask(rows * m - s0 - lat * rows - k * WL)
    r["K2"][...] = window_mask(half * m - s2 - lat * half)

    group = 4 if heads1 % 4 == 0 else heads1
    width = 3 * group * hd
    loads["wt"].wait()
    order = head_order(group, hd)
    for g in range(heads1 // group):
        cut = slice(g * width, (g + 1) * width)
        r["wt_o"][:, cut] = dot32(r["v_wt"][:, cut], order).astype(BF)
    for pd in range(pds):
        r["F"][pd] = dot32(r["B0"][...], flat(E[pd][0, :rows])).astype(BF)
    loads["b1"].wait()

    def fine_attention(pd):
        for cps in halo_copies:
            cps.one(pd).wait_recv()
        for k in range(wins):
            near = flat(E[pd][:, pl.ds(s0 + k * WL, WL)])
            framed = dot32(r["P1"][...], near)
            r["A"][pl.ds(k * WT, WT), :] = layer_norm(framed, r["g1"][...])
        r["tri"][...] = dot32(r["A"][...], r["wt_o"][...]).astype(BF)

        def one_group(g, carry):
            for k in range(wins):
                part = r["tri"][pl.ds(k * WT, WT), pl.ds(pl.multiple_of(g * width, 128), width)]
                total = attend(part, group, hd, lambda h: r["v_b1"][g * group + h], r["K1"][k])
                r["A"][pl.ds(k * WT, WT), pl.ds(pl.multiple_of(g * group * hd, 128), group * hd)] = (
                    total.astype(BF)
                )
            return carry

        lax.fori_loop(0, heads1 // group, one_group, 0)
        for k in range(wins):
            turned = dot32(r["U1"][...], r["A"][pl.ds(k * WT, WT), :])
            G[pd][0, pl.ds(HALO + k * WL, WL)] = turned.reshape(WL, seg, -1).astype(BF)
        for cps in back_copies[::-1]:
            cps.one(pd).start()

    for pd in range(pds):
        fine_attention(pd)

    for k in range(nz - 1):
        share_lon.one(k).wait_recv()
    for k in range(m - 1):
        share_lat.one(k).start()
    loads["wt2"].wait()
    swap(0).wait_recv()
    order = head_order(heads2, hd)
    for k in range(2):
        r["wt2_o"][k] = dot32(r["v_wt2"][k], order).astype(BF)
    for key in ("wo1", "we1", "wr1", "mw"):
        loads[key].wait()

    def fine_tail(pd):
        for cps in back_copies:
            cps.one(pd).wait_recv()
        r["near"][...] = flat(G[pd][:, pl.ds(HALO - s0, rows)])

        def some_rows(k, carry):
            at = pl.ds(pl.multiple_of(k * (cells // 2), 16), cells // 2)
            mixed = dot32(r["B1"][at, :], r["near"][...]).astype(BF)
            attended = (r["F"][pd, at, :].astype(F32) + dot32(mixed, r["v_wo1"][...])).astype(BF)
            normed = layer_norm(attended, r["gm"][...])
            hidden = jax.nn.gelu(dot32(normed, r["v_we1"][...])).astype(BF)
            state = (attended.astype(F32) + dot32(hidden, r["v_wr1"][...])).astype(BF)
            r["state"][pd, at, :] = state.astype(F32)
            return carry

        lax.fori_loop(0, 2, some_rows, 0)
        merged = jnp.concatenate([r["state"][pd, k * few : (k + 1) * few, :] for k in range(4)], axis=1)
        coarse_in = dot32(layer_norm(merged, r["mg"][...]), r["v_mw"][...]).astype(BF)
        r["cin"][pd] = coarse_in
        X[pd, zi] = layer_norm(coarse_in, r["g2"][...])
        gather1_start(pd)

    for pd in range(pds):
        fine_tail(pd)

    for pd in range(pds):
        for z in range(nz):
            Y[pd, core, z, few:] = pad

    def project(pd, z):
        given = X[pd, z]
        S[pd, z, pl.ds(0, few)] = dot32(given, r["wt2_o"][1 - core]).astype(BF)
        cross[0].one(pd, z).start()
        cross[2].one(pd, z).start()
        Y[pd, core, z, pl.ds(0, few)] = dot32(given, r["wt2_o"][core]).astype(BF)
        cross[1].one(pd, z).start()

    for pd in range(pds):
        project(pd, zi)
    both_streams(lambda pd, j: project(pd, gather1_arrive(pd, j)))
    for k in range(m - 1):
        share_lat.one(k).wait_recv()
    share_core.one(0).start()
    loads["b2"].wait()

    def coarse_attention(pd, carry):
        for z in range(nz):
            for cps in cross:
                cps.one(pd, z).wait_recv()

        def one_window(w, carry):
            zs = [lax.rem(w + dz, nz) for dz in range(2)]
            pieces = [Y[pd, par, z] for z in zs for par in range(2)]
            pieces += [H[pd, par, z] for z in zs for par in range(2)]
            part = dot32(r["P2"][...], jnp.concatenate(pieces, axis=0))
            total = attend(part, heads2, hd, lambda h: r["v_b2"][h], r["K2"][...])
            r["V"][w] = total.astype(BF)
            return carry

        lax.fori_loop(0, nz, one_window, 0)

        def one_chip(z, carry):
            both = jnp.concatenate([r["V"][z], r["V"][lax.rem(z + nz - 1, nz)]], axis=0)
            back = dot32(r["U2"][...], both).astype(BF)
            for par in range(2):
                C[pd, par, z] = back[par * fewp : (par + 1) * fewp]
                D[pd, par, z] = back[2 * fewp + par * hal : 2 * fewp + (par + 1) * hal]
            return carry

        lax.fori_loop(0, nz, one_chip, 0)
        for k in range(n):
            spread_next.one(pd, k).start()
        for k in range(n - 1):
            spread_here.one(pd, k).start()
        M[pd, lon] = C[pd, core, zi, pl.ds(0, few)]
        return carry

    coarse_attention(0, 0)
    coarse_attention(1, 0)
    share_core.one(0).wait_recv()

    def coarse_output(pd, carry):
        for k in range(n - 1):
            spread_here.one(pd, k).wait_recv()
        for k in range(n):
            spread_next.one(pd, k).wait_recv()
        value = r["cin"][pd].astype(F32)
        tail = jnp.zeros((few - hal, lanes2), F32)
        for g in range(n):
            part = M[pd, g].astype(F32) + jnp.concatenate([N[pd, g].astype(F32), tail], axis=0)
            rows_g = W[g % 2, :, g // 2]
            rows_g = rows_g.reshape(lanes2, -1) if rows_g.shape[1] % 16 == 0 else flat(rows_g)
            value += dot32(part.astype(BF), rows_g)
        middle = value.astype(BF)
        r["mid"][pd] = middle
        Z[pd, zi] = layer_norm(middle, r["gm2"][...])
        gather2_start(pd)
        return carry

    coarse_output(0, 0)
    coarse_output(1, 0)
    for key in ("we2", "wr2", "up"):
        loads[key].wait()
    swap(1).wait_recv()
    swap(2).wait_recv()

    def feed(pd, z):
        given = Z[pd, z]
        total = None
        for k in range(2):
            hidden = jax.nn.gelu(dot32(given, r["v_we2"][k])).astype(BF)
            term = dot32(hidden, r["v_wr2"][k])
            total = term if total is None else total + term
        return total

    def feed_step(pd, j):
        z = gather2_arrive(pd, j)
        term = feed(pd, z)

        @pl.when(adds(pd, z))
        def _():
            r["part"][pd, z] = term

        @pl.when(jnp.logical_not(adds(pd, z)))
        def _():
            Q[pd, z] = term.astype(BF)
            partial_start(pd, z)

    for pd in range(pds):
        r["own"][pd] = feed(pd, zi)
    both_streams(feed_step)
    for pd in range(pds):

        def pass_one(j, carry):
            partial_pass(pd, j)
            return carry

        lax.fori_loop(0, nz - 1, pass_one, 0)

    def finish(pd):
        r["sum"][...] = r["mid"][pd].astype(F32) + r["own"][pd]
        for way in range(3 if nz > 2 else 2):
            end = (zi == 0) | (zi == nz - 1)

            @pl.when((zi > 0, zi < nz - 1, end)[way])
            def _():
                pltpu.make_async_remote_copy(
                    Q.at[pd, zi],
                    T.at[pd, way],
                    r["rs0"].at[pd, zi],
                    r["rr0"].at[pd, way],
                    device_id=(lat, buddy),
                    device_id_type=MESH,
                ).wait_recv()
                r["sum"][...] = r["sum"][...] + T[pd, way].astype(F32)

        value = r["sum"][...]
        state = value.astype(BF)
        r["cstate"][pd] = state
        expanded = dot32(state, r["v_up"][...])
        channels = expanded.shape[1] // 4
        for k in range(4):
            at = slice(k * few, (k + 1) * few)
            cut = slice(k * channels, (k + 1) * channels)
            r["blended"][pd, at, :] = (r["state"][pd, at, :] + expanded[:, cut]).astype(BF)

    for pd in range(pds):
        finish(pd)

    for pd in range(pds):
        for cps in halo_copies + back_copies:
            cps.one(pd).wait_send()
        for z in range(nz):
            for cps in cross:
                cps.one(pd, z).wait_send()
        gather1_drain(pd)
        gather2_drain(pd)
        for k in range(1, nz):
            partial(pd, lax.rem(zi + k, nz))[1].wait_send()
        for k in range(n - 1):
            spread_here.one(pd, k).wait_send()
        for k in range(n):
            spread_next.one(pd, k).wait_send()
    for k in range(nz - 1):
        share_lon.one(k).wait_send()
    for k in range(m - 1):
        share_lat.one(k).wait_send()
    share_core.one(0).wait_send()
    for k in range(3):
        swap(k).wait_send()


def body(
    fine_field,
    offsets,
    fine_prenorm,
    fine_triple,
    fine_bias,
    fine_output,
    fine_midnorm,
    fine_expand,
    fine_reduce,
    merge_gain,
    merge_weight,
    coarse_prenorm,
    coarse_triple,
    coarse_bias,
    coarse_output,
    coarse_midnorm,
    coarse_expand,
    coarse_reduce,
    upsample_weight,
):
    levels, rows, cols, channels = fine_field.shape
    m = lax.axis_size("lat")
    n = lax.axis_size("lon")
    nz = n // 2
    pds = levels // WD
    wide = coarse_output.shape[1]
    heads1, heads2 = fine_bias.shape[0], coarse_bias.shape[0]
    hd = channels // heads1
    lanes2 = coarse_output.shape[0]
    assert cols == WW and rows == 2 * WL and n % 2 == 0 and nz >= 2 and pds == 2
    assert lanes2 == heads2 * hd and lanes2 % m == 0
    half, hc = rows // 2, cols // 2
    seg = WD * cols
    cells = rows * seg
    few = cells // 4
    fewp = up_to(few, 16)
    hal = up_to(HALO * WD * hc, 16)

    x = fine_field.transpose(1, 2, 0, 3)
    vmem = pl.BlockSpec(memory_space=pltpu.VMEM)
    hbm = pl.BlockSpec(memory_space=pl.ANY)
    args = [
        ("off", offsets, pl.BlockSpec(memory_space=pltpu.SMEM)),
        ("x", x, hbm),
        ("g1", fine_prenorm[None], vmem),
        ("wt", fine_triple, hbm),
        ("b1", fine_bias, hbm),
        ("wo1", fine_output, hbm),
        ("gm", fine_midnorm[None], vmem),
        ("we1", fine_expand, hbm),
        ("wr1", fine_reduce, hbm),
        ("mg", merge_gain[None], vmem),
        ("mw", merge_weight, hbm),
        ("g2", coarse_prenorm[None], vmem),
        ("wt2", coarse_triple, hbm),
        ("b2", coarse_bias, hbm),
        ("wo2", coarse_output.reshape(m, lanes2 // m, wide), hbm),
        ("gm2", coarse_midnorm[None], vmem),
        ("we2", coarse_expand, hbm),
        ("wr2", coarse_reduce, hbm),
        ("up", upsample_weight, hbm),
    ]
    outs = [
        ("blended", jax.ShapeDtypeStruct((pds, cells, channels), BF)),
        ("cstate", jax.ShapeDtypeStruct((pds, few, wide), BF)),
    ]
    sem = pltpu.SemaphoreType.DMA
    wide3 = 3 * lanes2
    scratch = [
        ("lsem", sem((14,))),
        ("v_wt", pltpu.VMEM(fine_triple.shape, BF)),
        ("wt_o", pltpu.VMEM(fine_triple.shape, BF)),
        ("v_b1", pltpu.VMEM(fine_bias.shape, F32)),
        ("v_wo1", pltpu.VMEM(fine_output.shape, BF)),
        ("v_we1", pltpu.VMEM(fine_expand.shape, BF)),
        ("v_wr1", pltpu.VMEM(fine_reduce.shape, BF)),
        ("v_mw", pltpu.VMEM(merge_weight.shape, BF)),
        ("v_wt2", pltpu.VMEM((2,) + coarse_triple.shape, BF)),
        ("wt2_o", pltpu.VMEM((2,) + coarse_triple.shape, BF)),
        ("v_b2", pltpu.VMEM(coarse_bias.shape, F32)),
        ("v_we2", pltpu.VMEM((2,) + coarse_expand.shape, BF)),
        ("v_wr2", pltpu.VMEM((2,) + coarse_reduce.shape, BF)),
        ("v_up", pltpu.VMEM(upsample_weight.shape, BF)),
        ("W", pltpu.VMEM((2, m, nz, lanes2 // m, wide), BF)),
        ("P1", pltpu.VMEM((WT, 2 * WL * seg), BF)),
        ("U1", pltpu.VMEM((WT, WT), BF)),
        ("B0", pltpu.VMEM((cells, cells), BF)),
        ("B1", pltpu.VMEM((cells, 2 * cells), BF)),
        ("v_x", pltpu.VMEM(x.shape, BF)),
        ("P2", pltpu.VMEM((WT, 4 * fewp + 4 * hal), BF)),
        ("U2", pltpu.VMEM((2 * fewp + 2 * hal, 2 * WT), BF)),
        ("K1", pltpu.VMEM((rows // WL, WT, WT), F32)),
        ("K2", pltpu.VMEM((WT, WT), F32)),
        ("F", pltpu.VMEM((pds, cells, channels), BF)),
        ("A", pltpu.VMEM((cells, channels), BF)),
        ("tri", pltpu.VMEM((cells, 3 * channels), BF)),
        ("near", pltpu.VMEM((2 * cells, channels), BF)),
        ("state", pltpu.VMEM((pds, cells, channels), F32)),
        ("cin", pltpu.VMEM((pds, few, wide), BF)),
        ("X", pltpu.VMEM((pds, nz, few, wide), BF)),
        ("Y", pltpu.VMEM((pds, 2, nz, fewp, wide3), BF)),
        ("S", pltpu.VMEM((pds, nz, fewp, wide3), BF)),
        ("H", pltpu.VMEM((pds, 2, nz, hal, wide3), BF)),
        ("V", pltpu.VMEM((nz, WT, lanes2), BF)),
        ("C", pltpu.VMEM((pds, 2, nz, fewp, lanes2), BF)),
        ("D", pltpu.VMEM((pds, 2, nz, hal, lanes2), BF)),
        ("M", pltpu.VMEM((pds, n, few, lanes2), BF)),
        ("N", pltpu.VMEM((pds, n, hal, lanes2), BF)),
        ("mid", pltpu.VMEM((pds, few, wide), BF)),
        ("Z", pltpu.VMEM((pds, nz, few, wide), BF)),
        ("own", pltpu.VMEM((pds, few, wide), F32)),
        ("Q", pltpu.VMEM((pds, nz, few, wide), BF)),
        ("T", pltpu.VMEM((pds, 3, few, wide), BF)),
        ("R", pltpu.VMEM((pds, nz, few, wide), BF)),
        ("part", pltpu.VMEM((pds, nz, few, wide), F32)),
        ("sum", pltpu.VMEM((few, wide), F32)),
    ]
    for pd in range(pds):
        for name in ("E", "G"):
            scratch.append((name + str(pd), pltpu.VMEM((2, rows + HALO, seg, channels), BF)))
    for name, shape in (("h", (pds,)), ("b", (pds,)), ("c", (pds, nz))):
        for k in range(3):
            scratch += [("%ss%d" % (name, k), sem(shape)), ("%sr%d" % (name, k), sem(shape))]
    for s, d, shape in (
        ("ws0", "wr0", (nz - 1,)),
        ("ws1", "wr1s", (m - 1,)),
        ("ws2", "wr2s", (1,)),
        ("ss", "sr", (3,)),
        ("as0", "ar0", (pds, 2, nz - 1)),
        ("as1", "ar1", (pds, 2, nz - 1)),
        ("ds0", "dr0", (pds, n - 1)),
        ("ds1", "dr1", (pds, n)),
    ):
        scratch += [(s, sem(shape)), (d, sem(shape))]
    scratch += [("rs0", sem((pds, nz))), ("rr0", sem((pds, 3))), ("rr1", sem((pds, nz)))]

    cfg = dict(m=m, n=n, pds=pds, rows=rows, cols=cols, heads1=heads1, heads2=heads2, hd=hd)
    names = [a[0] for a in args] + [o[0] for o in outs] + [s[0] for s in scratch]
    blended, state = pl.pallas_call(
        functools.partial(step_kernel, cfg, names),
        out_shape=[o[1] for o in outs],
        in_specs=[a[2] for a in args],
        out_specs=[vmem, vmem],
        scratch_shapes=[s[1] for s in scratch],
        compiler_params=pltpu.CompilerParams(
            collective_id=0, has_side_effects=True, vmem_limit_bytes=63 << 20
        ),
    )(*[a[1] for a in args])
    blended, state = pl.pallas_call(
        arrange_kernel,
        out_shape=[
            jax.ShapeDtypeStruct(x.shape, BF),
            jax.ShapeDtypeStruct((half, hc, levels, wide), BF),
        ],
        in_specs=[vmem, vmem],
        out_specs=[vmem, vmem],
    )(blended, state)
    return blended.transpose(2, 0, 1, 3), state.transpose(2, 0, 1, 3)


def solution(mesh):
    placed = (
        P(None, "lat", "lon", None),
        P(),
        P(),
        P(),
        P(),
        P(),
        P(),
        P(),
        P(),
        P(),
        P(),
        P(),
        P(None, "lon"),
        P("lon", None, None),
        P("lon", None),
        P(),
        P(None, "lon"),
        P("lon", None),
        P(),
    )
    return jax.shard_map(
        body,
        mesh=mesh,
        in_specs=placed,
        out_specs=(P(None, "lat", "lon", None), P(None, "lat", "lon", None)),
        check_vma=False,
    )
```
